32 devices in a mesh: expert: 4 (over y, core), space: 8 (over z, x).
Axes of the slice: x: 2, y: 2, z: 4, core: 2. Of those that a mesh axis runs over, the one named last changes fastest.
Arguments:
- attn_inputs: bfloat16 [3, 4, 96, 12, 512], P(None, 'expert', 'space'), may hold values from -9 to 9
- residual: bfloat16 [4, 96, 12, 512], P('expert', 'space'), may hold values from -400 to 400
- logits: float32 [4, 96, 12, 32], P('expert', 'space'), may hold values from -12 to 454
- expert_ids: int32 [4, 96, 12, 2], P('expert', 'space'), may hold values from 0 to 31, all different within a row; in each aligned block of 144 rows (0 to 143, 144 to 287, ..., all dimensions but the last counted through in order) at most 12 rows name the same one
- keep_mask: int32 [4, 96, 12, 2], P('expert', 'space'), may hold values 0 or 1
- cotangent: bfloat16 [4, 96, 12, 512], P('expert', 'space'), may hold values from -1.5 to 1.5
- up_weight: bfloat16 [32, 512, 2048], P('expert', None, 'space'), may hold values from -0.25 to 0.25
- down_weight: bfloat16 [32, 512, 2048], P('expert', None, 'space'), may hold values from -0.125 to 0.125
Outputs:
- attn_grad: bfloat16 [3, 4, 96, 12, 512], P(None, 'expert', 'space')
- residual_grad: bfloat16 [4, 96, 12, 512], P('expert', 'space')
- up_grad: float32 [32, 512, 2048], P('expert', None, 'space')
- down_grad: float32 [32, 512, 2048], P('expert', None, 'space')
- logit_grad: float32 [4, 96, 12, 32], P('expert', 'space')
The draws below stay inside these ranges and needn't reach their ends.
Inputs may be any that keep to these rules, and one draw needn't show every extreme that they name: `expert_ids`: each token names 2 different experts; among the tokens of one strip no expert is named more than 12 times, and in every draw some expert is named exactly 12 times by the tokens of some strip.
All inputs are finite; a program needn't handle non-finite values. No bound on the sum of `keep_mask` on one device may be relied on, other than what follows from the above.
Results may differ from the reference program's by a relative error of at most 0.012.
Values may be sent and summed in bfloat16 or wider, within the bound.
No kernel may reach another device: no remote copies, remote signals or barrier semaphores. Data moves between devices by JAX's collectives and lax.ppermute only.
A program may use at most 128 MiB of HBM per device.

```python
import math
import jax
import jax.numpy as jnp
import numpy as np
from jax import lax

C = 512
HEADS = 16
F = 2048
EXPERTS = 32
WIN = 12
TOP = 2
WW = 12
SHIFT = 6
NIMG = 4
IMG_H = 96
TOK_DEV = 144
CAP = 12
N_SPACE = 8


def draw_attn_inputs(key, part):
    full_shape = (3, NIMG, IMG_H, WW, C)
    key_base = jax.random.fold_in(key, 0)
    base_draw = jnp.clip(jax.random.normal(key_base, full_shape, jnp.float32), -4.0, 4.0)
    return base_draw.astype(jnp.bfloat16)


def draw_residual(key, part):
    full_shape = (NIMG, IMG_H, WW, C)
    key_base, key_rows, key_cols = jax.random.split(key, 3)
    base_draw = jnp.clip(jax.random.normal(key_base, full_shape, jnp.float32), -4.0, 4.0)
    row_scale = jnp.exp(jax.random.uniform(key_rows, (NIMG, IMG_H, WW, 1), jnp.float32, 0.0, math.log(10.0)))
    col_scale = jnp.exp(jax.random.uniform(key_cols, (C,), jnp.float32, 0.0, math.log(10.0)))
    return (base_draw * row_scale * col_scale).astype(jnp.bfloat16)


def draw_logits(key, part):
    full_shape = (NIMG, IMG_H, WW, EXPERTS)
    key_base = jax.random.fold_in(key, 0)
    base_draw = jnp.clip(3.0 * jax.random.normal(key_base, full_shape, jnp.float32), -12.0, 12.0)
    return base_draw


def set_ends(entries, rng, smallest, largest):
    longest = entries.shape.index(max(entries.shape))
    spots = []
    for shift in (0, 1):
        where = [jax.random.randint(jax.random.fold_in(rng, axis), (), 0, length) for axis, length in enumerate(entries.shape)]
        where[longest] = (where[longest] + shift) % entries.shape[longest]
        spots.append(tuple(where))
    return entries.at[spots[0]].set(smallest).at[spots[1]].set(largest)


def steps_of(own_key, extent, pieces, smallest, top_value):
    factor_of = 1.0
    for axis_at, shards_of in pieces:
        heights = jax.random.uniform(jax.random.fold_in(jax.random.fold_in(own_key, 6), axis_at), (shards_of,), jnp.float32, smallest / len(pieces), top_value / len(pieces))
        factor_of = factor_of * jnp.repeat(jnp.exp(heights), extent[axis_at] // shards_of).reshape((-1,) + (1,) * (len(extent) - 1 - axis_at))
    return factor_of


def assign_block(stream_key, own, number, rows, count, top, limit, lean):
    sequence = jax.random.permutation(stream_key, count)
    packed, common = load_shares(count, rows * top, limit, lean, True), load_shares(count, rows * top, limit, lean, False)
    places = jnp.arange(count)

    def named(sizes, offset_by):
        used = int((sizes > 0).sum())
        fixed = max(1, used // 4)
        shifted = fixed + (places - fixed + offset_by * (used - fixed)) % max(1, count - fixed)
        return jnp.zeros((count,), jnp.int32).at[sequence[jnp.where(places < fixed, places, shifted)]].set(jnp.asarray(sizes, jnp.int32))

    sizes = jnp.where(number % 4 == 0, named(packed, number // 4), named(common, number - number // 4 - 1))
    mixed = jax.random.permutation(jax.random.fold_in(own, 3), count)
    giver, receiver = mixed[0:count // 2 * 2:2], mixed[1:count // 2 * 2:2]
    margin = jnp.minimum(sizes[giver] - 1, limit - sizes[receiver]) // 2
    margin = jnp.where((giver == sequence[0]) | (receiver == sequence[0]) | (sizes[receiver] == 0), 0, jnp.maximum(margin, 0))
    shifted = jax.random.randint(jax.random.fold_in(own, 4), (count // 2,), 0, 1 << 20) % (margin + 1)
    sizes = sizes.at[giver].add(-shifted).at[receiver].add(shifted)
    labels = jnp.searchsorted(jnp.cumsum(sizes), jnp.arange(rows * top), side="right").astype(jnp.int32)
    table = labels.reshape(top, rows).T
    table = table[jax.random.permutation(jax.random.fold_in(own, 1), rows)]
    offset_by = jax.random.randint(jax.random.fold_in(own, 2), (rows, 1), 0, top)
    return jnp.take_along_axis(table, (jnp.arange(top)[None, :] + offset_by) % top, axis=1)


def load_shares(count, total, most, lean, full):
    weights = [(1 << 20) // math.isqrt(rank ** lean) + 1 for rank in range(1, count + 1)]
    largest = most if full else min(most, max(-(-total // count), total * weights[0] // sum(weights)))
    least = 1 if total - largest >= count - 1 else 0
    holding, spare = [largest] + [least] * (count - 1), total - largest - least * (count - 1)
    while spare > 0:
        movable = [i for i in range(1, count) if holding[i] < largest] or [i for i in range(1, count) if holding[i] < most]
        whole, remaining = sum([weights[i] for i in movable]), spare
        for i in movable:
            addition = min(most - holding[i], max(1, remaining * weights[i] // whole), spare)
            holding[i] = holding[i] + addition
            spare = spare - addition
    return np.array(holding)


def centred(key, dims, deviation, most, cuts=(), held_as=jnp.bfloat16):
    result = deviation * jax.random.normal(key, dims, jnp.float32)
    if cuts:
        result = result * steps_of(key, dims, cuts, -0.22, 0.18)
    return jnp.clip(result, -most, most).astype(held_as)


def setup_inputs(seed: int = 0) -> dict:
    key_of = jax.random.split(jax.random.key(seed), 9)
    attn_inputs = draw_attn_inputs(jax.random.fold_in(key_of[8], 71), 0)
    residual = draw_residual(jax.random.fold_in(key_of[8], 71), 0)
    logits = draw_logits(jax.random.fold_in(key_of[8], 71), 0)
    expert_ids_keys = jax.random.split(jax.random.fold_in(key_of[3], 1), NIMG * IMG_H * WW // TOK_DEV)
    expert_ids_turns = jax.random.permutation(jax.random.fold_in(key_of[3], 3), NIMG * IMG_H * WW // TOK_DEV)
    expert_ids = jax.vmap(lambda own, number: assign_block(jax.random.fold_in(key_of[3], 2), own, number, TOK_DEV, EXPERTS, TOP, CAP, 1))(expert_ids_keys, expert_ids_turns).reshape((NIMG, IMG_H, WW, TOP))
    keep_mask = set_ends((jax.random.randint(key_of[4], (NIMG, IMG_H, WW, TOP), 0, 16) < 15).astype(jnp.int32), jax.random.fold_in(key_of[4], 1), 0, 1)
    cotangent = centred(key_of[5], (NIMG, IMG_H, WW, C), 0.25, 1.5, ((0, 4), (1, 8)))
    up_weight = centred(key_of[6], (EXPERTS, C, F), C ** -0.5, 0.25, ((0, 4), (2, 8)))
    down_weight = centred(key_of[7], (EXPERTS, C, F), F ** -0.5, 0.125, ((0, 4), (2, 8)))
    return dict(attn_inputs=attn_inputs, residual=residual, logits=logits, expert_ids=expert_ids, keep_mask=keep_mask, cotangent=cotangent, up_weight=up_weight, down_weight=down_weight)


NORM_EPS = 1e-06
SCORE_MASK = -100.0

def gelu_pair(pre_act):
    activation, pullback = jax.vjp(jax.nn.gelu, pre_act)
    gelu_slope = pullback(jnp.ones_like(pre_act))[0]
    return (activation, gelu_slope)

def to_windows(tensor, head_count):
    blocks, win_side, map_width, channels = tensor.shape
    win_count = map_width // win_side
    head_dim = channels // head_count
    shaped = tensor.reshape(blocks, win_side, win_count, win_side, head_count, head_dim)
    shaped = shaped.transpose(0, 2, 4, 1, 3, 5)
    return shaped.reshape(blocks, win_count, head_count, win_side * win_side, head_dim)

def from_windows(tensor, win_side):
    blocks, win_count, head_count, win_area, head_dim = tensor.shape
    shaped = tensor.reshape(blocks, win_count, head_count, win_side, win_side, head_dim)
    shaped = shaped.transpose(0, 3, 1, 4, 2, 5)
    return shaped.reshape(blocks, win_side, win_count * win_side, head_count * head_dim)

def window_grads(frame_qkv, frame_grad, last_flags, head_count):
    win_side = frame_grad.shape[1]
    map_width = frame_grad.shape[2]
    half_win = win_side // 2
    head_dim = frame_grad.shape[3] // head_count
    inv_sqrt = head_dim ** (-0.5)
    highest = lax.Precision.HIGHEST
    rolled = jnp.roll(frame_qkv, -half_win, axis=3)
    grad_rolled = jnp.roll(frame_grad, -half_win, axis=2)
    query_win = to_windows(rolled[0], head_count).astype(jnp.float32)
    key_win = to_windows(rolled[1], head_count).astype(jnp.float32)
    value_win = to_windows(rolled[2], head_count).astype(jnp.float32)
    grad_win = to_windows(grad_rolled, head_count).astype(jnp.float32)
    row_pos = jnp.arange(win_side, dtype=jnp.int32)
    col_pos = jnp.arange(map_width, dtype=jnp.int32)
    row_label = jnp.where(last_flags[:, None], jnp.where(row_pos < half_win, 1, 2)[None, :], 0)
    col_label = jnp.where(col_pos >= map_width - win_side, jnp.where(col_pos < map_width - half_win, 1, 2), 0)
    region = 3 * row_label[:, :, None] + col_label[None, None, :]
    region = region.reshape(region.shape[0], win_side, map_width // win_side, win_side).transpose(0, 2, 1, 3)
    region = region.reshape(region.shape[0], region.shape[1], win_side * win_side)
    score_bias = jnp.where(region[:, :, :, None] != region[:, :, None, :], SCORE_MASK, 0.0)[:, :, None]
    scores = jnp.einsum('bnhqd,bnhkd->bnhqk', query_win, key_win, precision=highest) * inv_sqrt + score_bias
    row_max = lax.optimization_barrier(jnp.max(scores, axis=-1, keepdims=True))
    exp_scores = jnp.exp(scores - row_max)
    attn_probs = exp_scores / lax.optimization_barrier(jnp.sum(exp_scores, axis=-1, keepdims=True))
    weights_bf = attn_probs.astype(jnp.bfloat16).astype(jnp.float32)
    attn_out = jnp.einsum('bnhqk,bnhkd->bnhqd', weights_bf, value_win, precision=highest)
    row_delta = lax.optimization_barrier(jnp.sum(grad_win * attn_out, axis=-1, keepdims=True))
    prob_grad = jnp.einsum('bnhqd,bnhkd->bnhqk', grad_win, value_win, precision=highest)
    score_grad = (attn_probs * (prob_grad - row_delta)).astype(jnp.bfloat16).astype(jnp.float32)
    query_grad = (jnp.einsum('bnhqk,bnhkd->bnhqd', score_grad, key_win, precision=highest) * inv_sqrt).astype(jnp.bfloat16)
    key_grad = (jnp.einsum('bnhqk,bnhqd->bnhkd', score_grad, query_win, precision=highest) * inv_sqrt).astype(jnp.bfloat16)
    value_grad = jnp.einsum('bnhqk,bnhqd->bnhkd', weights_bf, grad_win, precision=highest).astype(jnp.bfloat16)
    stacked = jnp.stack([from_windows(query_grad, win_side), from_windows(key_grad, win_side), from_windows(value_grad, win_side)])
    return jnp.roll(stacked, half_win, axis=3)

def expert_pass(operands):
    in_rows, cot_rows, scaled, up_mat, down_mat = operands
    pre_act = jnp.dot(in_rows, up_mat, preferred_element_type=jnp.float32)
    activation, gelu_slope = gelu_pair(pre_act)
    act_bf = activation.astype(jnp.bfloat16)
    expert_out = jnp.dot(act_bf, down_mat.T, preferred_element_type=jnp.float32)
    row_dots = lax.optimization_barrier(jnp.sum(cot_rows.astype(jnp.float32) * expert_out, axis=-1)).astype(jnp.bfloat16)
    pre_grad = (jnp.dot(scaled, down_mat, preferred_element_type=jnp.float32) * gelu_slope).astype(jnp.bfloat16)
    row_grad = jnp.dot(pre_grad, up_mat.T, preferred_element_type=jnp.float32).astype(jnp.bfloat16)
    up_part = jnp.dot(in_rows.T, pre_grad, preferred_element_type=jnp.float32)
    down_part = jnp.dot(scaled.T, act_bf, preferred_element_type=jnp.float32)
    return (row_grad, row_dots, up_part, down_part)

def reference(attn_inputs, residual, logits, expert_ids, keep_mask, cotangent, up_weight, down_weight):
    groups_total = NIMG * N_SPACE
    resid_float = residual.reshape(groups_total, TOK_DEV, C).astype(jnp.float32)
    rms_value = jnp.sqrt(lax.optimization_barrier(jnp.mean(resid_float * resid_float, axis=-1, keepdims=True)) + NORM_EPS)
    norm_float = resid_float / rms_value
    normed = norm_float.astype(jnp.bfloat16)
    route_ids = expert_ids.reshape(groups_total, TOK_DEV, TOP)
    keep_float = keep_mask.reshape(groups_total, TOK_DEV, TOP).astype(jnp.float32)
    router_logits = logits.reshape(groups_total, TOK_DEV, EXPERTS)
    expert_cols = jnp.arange(EXPERTS, dtype=jnp.int32)
    one_hot = route_ids[..., None] == expert_cols
    chosen = lax.optimization_barrier(jnp.sum(jnp.where(one_hot, router_logits[:, :, None, :], 0.0), axis=-1))
    chosen_max = lax.optimization_barrier(jnp.max(chosen, axis=-1, keepdims=True))
    chosen_exp = jnp.exp(chosen - chosen_max)
    gates_top = chosen_exp / lax.optimization_barrier(jnp.sum(chosen_exp, axis=-1, keepdims=True))
    gate_weight = gates_top * keep_float
    cot_rows = cotangent.reshape(groups_total, TOK_DEV, C)
    scaled_rows = (gate_weight[..., None] * cot_rows[:, :, None, :].astype(jnp.float32)).astype(jnp.bfloat16)
    flat_hot = one_hot.reshape(groups_total, TOK_DEV * TOP, EXPERTS).astype(jnp.int32)
    running = (jnp.cumsum(flat_hot, axis=1) - flat_hot).astype(jnp.int32)
    slot_index = lax.optimization_barrier(jnp.sum(running * flat_hot, axis=-1)).astype(jnp.int32)
    flat_ids = route_ids.reshape(groups_total, TOK_DEV * TOP).astype(jnp.int32)
    group_index = jnp.arange(groups_total, dtype=jnp.int32)[:, None]
    destination = ((flat_ids * groups_total + group_index) * CAP + slot_index).reshape(-1).astype(jnp.int32)
    slot_total = EXPERTS * groups_total * CAP
    expert_rows = groups_total * CAP
    choice_norm = jnp.broadcast_to(normed[:, :, None, :], (groups_total, TOK_DEV, TOP, C)).reshape(-1, C)
    choice_cot = jnp.broadcast_to(cot_rows[:, :, None, :], (groups_total, TOK_DEV, TOP, C)).reshape(-1, C)
    norm_buffer = jnp.zeros((slot_total, C), jnp.bfloat16).at[destination].set(choice_norm)
    cot_buffer = jnp.zeros((slot_total, C), jnp.bfloat16).at[destination].set(choice_cot)
    scaled_buffer = jnp.zeros((slot_total, C), jnp.bfloat16).at[destination].set(scaled_rows.reshape(-1, C))
    row_grad, row_dots, up_grad, down_grad = lax.map(expert_pass, (norm_buffer.reshape(EXPERTS, expert_rows, C), cot_buffer.reshape(EXPERTS, expert_rows, C), scaled_buffer.reshape(EXPERTS, expert_rows, C), up_weight, down_weight))
    choice_grad = row_grad.reshape(slot_total, C)[destination].astype(jnp.float32).reshape(groups_total, TOK_DEV, TOP, C)
    norm_grad = lax.optimization_barrier(jnp.sum(choice_grad, axis=2))
    inner_mean = lax.optimization_barrier(jnp.mean(norm_grad * norm_float, axis=-1, keepdims=True))
    residual_grad = (cot_rows.astype(jnp.float32) + (norm_grad - norm_float * inner_mean) / rms_value).astype(jnp.bfloat16)
    choice_dots = row_dots.reshape(slot_total)[destination].astype(jnp.float32).reshape(groups_total, TOK_DEV, TOP)
    gate_drive = keep_float * choice_dots
    gate_mix = lax.optimization_barrier(jnp.sum(gates_top * gate_drive, axis=-1, keepdims=True))
    gate_part = gates_top * (gate_drive - gate_mix)
    logit_gate = lax.optimization_barrier(jnp.sum(jnp.where(one_hot, gate_part[..., None], 0.0), axis=2))
    expert_share = lax.optimization_barrier(jnp.sum(jnp.where(one_hot, keep_float[..., None], 0.0), axis=(1, 2))) / (TOP * TOK_DEV)
    logit_max = lax.optimization_barrier(jnp.max(router_logits, axis=-1, keepdims=True))
    logit_exp = jnp.exp(router_logits - logit_max)
    router_probs = logit_exp / lax.optimization_barrier(jnp.sum(logit_exp, axis=-1, keepdims=True))
    share_mean = lax.optimization_barrier(jnp.sum(router_probs * expert_share[:, None, :], axis=-1, keepdims=True))
    balance = EXPERTS * router_probs * (expert_share[:, None, :] - share_mean)
    logit_grad = (logit_gate + balance).reshape(NIMG, IMG_H, WW, EXPERTS)
    residual_map = residual_grad.reshape(NIMG, IMG_H, WW, C)
    last_flags = jnp.arange(N_SPACE, dtype=jnp.int32) == N_SPACE - 1

    def image_pass(operands):
        image_qkv, image_grad = operands
        frame_qkv = jnp.roll(image_qkv, -SHIFT, axis=1).reshape(3, N_SPACE, WIN, WW, C)
        frame_grad = jnp.roll(image_grad, -SHIFT, axis=0).reshape(N_SPACE, WIN, WW, C)
        frame_grads = window_grads(frame_qkv, frame_grad, last_flags, HEADS)
        return jnp.roll(frame_grads.reshape(3, IMG_H, WW, C), SHIFT, axis=1)
    image_grads = lax.map(image_pass, (jnp.moveaxis(attn_inputs, 1, 0), residual_map))
    attn_grad = jnp.moveaxis(image_grads, 0, 1)
    return (attn_grad, residual_map, up_grad, down_grad, logit_grad)
```

```python
import jax
import jax.numpy as jnp
from jax import lax
from jax.sharding import PartitionSpec as P

HEADS = 16
EXPERTS = 32
TOP = 2
CAP = 12


NORM_EPS = 1e-06
SCORE_MASK = -100.0


def from_behind(block, axis, distance):
    devices = range(lax.axis_size(axis))
    route = [((i - distance) % len(devices), i) for i in devices]
    return lax.ppermute(block, axis, route)


def gelu_pair(pre_act):
    activation, pullback = jax.vjp(jax.nn.gelu, pre_act)
    gelu_slope = pullback(jnp.ones_like(pre_act))[0]
    return (activation, gelu_slope)


def to_windows(tensor, head_count):
    blocks, win_side, map_width, channels = tensor.shape
    win_count = map_width // win_side
    head_dim = channels // head_count
    shaped = tensor.reshape(blocks, win_side, win_count, win_side, head_count, head_dim)
    shaped = shaped.transpose(0, 2, 4, 1, 3, 5)
    return shaped.reshape(blocks, win_count, head_count, win_side * win_side, head_dim)


def from_windows(tensor, win_side):
    blocks, win_count, head_count, win_area, head_dim = tensor.shape
    shaped = tensor.reshape(blocks, win_count, head_count, win_side, win_side, head_dim)
    shaped = shaped.transpose(0, 3, 1, 4, 2, 5)
    return shaped.reshape(blocks, win_side, win_count * win_side, head_count * head_dim)


def window_grads(frame_qkv, frame_grad, last_flags, head_count):
    win_side = frame_grad.shape[1]
    map_width = frame_grad.shape[2]
    half_win = win_side // 2
    head_dim = frame_grad.shape[3] // head_count
    inv_sqrt = head_dim ** (-0.5)
    rolled = jnp.roll(frame_qkv, -half_win, axis=3)
    grad_rolled = jnp.roll(frame_grad, -half_win, axis=2)
    query_win = to_windows(rolled[0], head_count)
    key_win = to_windows(rolled[1], head_count)
    value_win = to_windows(rolled[2], head_count)
    grad_win = to_windows(grad_rolled, head_count)
    row_pos = jnp.arange(win_side, dtype=jnp.int32)
    col_pos = jnp.arange(map_width, dtype=jnp.int32)
    row_label = jnp.where(last_flags[:, None], jnp.where(row_pos < half_win, 1, 2)[None, :], 0)
    col_label = jnp.where(
        col_pos >= map_width - win_side, jnp.where(col_pos < map_width - half_win, 1, 2), 0
    )
    region = 3 * row_label[:, :, None] + col_label[None, None, :]
    region = region.reshape(region.shape[0], win_side, map_width // win_side, win_side).transpose(
        0, 2, 1, 3
    )
    region = region.reshape(region.shape[0], region.shape[1], win_side * win_side)
    score_bias = jnp.where(region[:, :, :, None] != region[:, :, None, :], SCORE_MASK, 0.0)[
        :, :, None
    ]
    scores = (
        jnp.einsum("bnhqd,bnhkd->bnhqk", query_win, key_win, preferred_element_type=jnp.float32)
        * inv_sqrt
        + score_bias
    )
    row_max = jnp.max(scores, axis=-1, keepdims=True)
    exp_scores = jnp.exp(scores - row_max)
    attn_probs = exp_scores / jnp.sum(exp_scores, axis=-1, keepdims=True)
    weights_bf = attn_probs.astype(jnp.bfloat16)
    attn_out = jnp.einsum(
        "bnhqk,bnhkd->bnhqd", weights_bf, value_win, preferred_element_type=jnp.float32
    )
    row_delta = jnp.sum(grad_win.astype(jnp.float32) * attn_out, axis=-1, keepdims=True)
    prob_grad = jnp.einsum(
        "bnhqd,bnhkd->bnhqk", grad_win, value_win, preferred_element_type=jnp.float32
    )
    score_grad = (attn_probs * (prob_grad - row_delta)).astype(jnp.bfloat16)
    query_grad = (
        jnp.einsum("bnhqk,bnhkd->bnhqd", score_grad, key_win, preferred_element_type=jnp.float32)
        * inv_sqrt
    ).astype(jnp.bfloat16)
    key_grad = (
        jnp.einsum("bnhqk,bnhqd->bnhkd", score_grad, query_win, preferred_element_type=jnp.float32)
        * inv_sqrt
    ).astype(jnp.bfloat16)
    value_grad = jnp.einsum(
        "bnhqk,bnhqd->bnhkd", weights_bf, grad_win, preferred_element_type=jnp.float32
    ).astype(jnp.bfloat16)
    stacked = jnp.stack(
        [
            from_windows(query_grad, win_side),
            from_windows(key_grad, win_side),
            from_windows(value_grad, win_side),
        ]
    )
    return jnp.roll(stacked, half_win, axis=3)


def per_device(
    attn_inputs, residual, logits, expert_ids, keep_mask, cotangent, up_weight, down_weight
):
    group_count = lax.axis_size("expert")
    local_experts = up_weight.shape[0]
    win_side = residual.shape[1]
    map_width = residual.shape[2]
    channels = residual.shape[3]
    tokens = win_side * map_width
    half_win = win_side // 2
    space_index = lax.axis_index("space")
    space_count = lax.axis_size("space")
    qkv_local = attn_inputs[:, 0]
    next_rows = from_behind(qkv_local[:, :half_win], "space", -1)
    qkv_shifted = jnp.concatenate([qkv_local[:, half_win:], next_rows], axis=1)
    resid_float = residual[0].reshape(tokens, channels).astype(jnp.float32)
    rms_value = jnp.sqrt(jnp.mean(resid_float * resid_float, axis=-1, keepdims=True) + NORM_EPS)
    norm_float = resid_float / rms_value
    normed = norm_float.astype(jnp.bfloat16)
    route_ids = expert_ids[0].reshape(tokens, TOP)
    keep_float = keep_mask[0].reshape(tokens, TOP).astype(jnp.float32)
    router_logits = logits[0].reshape(tokens, EXPERTS)
    expert_cols = jnp.arange(EXPERTS, dtype=jnp.int32)
    one_hot = route_ids[:, :, None] == expert_cols[None, None, :]
    chosen = jnp.sum(jnp.where(one_hot, router_logits[:, None, :], 0.0), axis=-1)
    chosen_max = jnp.max(chosen, axis=-1, keepdims=True)
    chosen_exp = jnp.exp(chosen - chosen_max)
    gates_top = chosen_exp / jnp.sum(chosen_exp, axis=-1, keepdims=True)
    gate_weight = gates_top * keep_float
    cot_rows = cotangent[0].reshape(tokens, channels)
    flat_hot = one_hot.reshape(tokens * TOP, EXPERTS).astype(jnp.int32)
    running = jnp.cumsum(flat_hot, axis=0) - flat_hot
    slot_index = jnp.sum(running * flat_hot, axis=-1)
    flat_ids = route_ids.reshape(-1)
    destination = (
        flat_ids % local_experts * group_count + flat_ids // local_experts
    ) * CAP + slot_index
    slot_total = local_experts * group_count * CAP
    choice_norm = jnp.broadcast_to(normed[:, None, :], (tokens, TOP, channels)).reshape(
        tokens * TOP, channels
    )
    choice_cot = jnp.broadcast_to(cot_rows[:, None, :], (tokens, TOP, channels)).reshape(
        tokens * TOP, channels
    )
    send_norm = (
        jnp.zeros((slot_total, channels), jnp.bfloat16)
        .at[destination]
        .set(choice_norm)
        .reshape(local_experts, group_count, CAP, channels)
    )
    send_cot = (
        jnp.zeros((slot_total, channels), jnp.bfloat16)
        .at[destination]
        .set(choice_cot)
        .reshape(local_experts, group_count, CAP, channels)
    )
    send_gate = (
        jnp.zeros((slot_total,), jnp.float32)
        .at[destination]
        .set(gate_weight.reshape(tokens * TOP))
        .reshape(local_experts, group_count, CAP)
    )
    recv_norm, recv_cot, recv_gate = (
        lax.all_to_all(send_norm, "expert", split_axis=1, concat_axis=1, tiled=True),
        lax.all_to_all(send_cot, "expert", split_axis=1, concat_axis=1, tiled=True),
        lax.all_to_all(send_gate, "expert", split_axis=1, concat_axis=1, tiled=True),
    )
    expert_rows = group_count * CAP
    in_rows = recv_norm.reshape(local_experts, expert_rows, channels)
    cot_in = recv_cot.reshape(local_experts, expert_rows, channels)
    gate_in = recv_gate.reshape(local_experts, expert_rows)
    norm_piece = lax.all_gather(in_rows, "space", axis=1, tiled=True)
    cot_piece = lax.all_gather(cot_in, "space", axis=1, tiled=True)
    gate_piece = lax.all_gather(gate_in, "space", axis=1, tiled=True)[:, :, None]
    pre_own = jnp.einsum("erc,ecf->erf", norm_piece, up_weight, preferred_element_type=jnp.float32)
    act_own, slope_own = gelu_pair(pre_own)
    drive = jnp.einsum("erc,ecf->erf", cot_piece, down_weight, preferred_element_type=jnp.float32)
    act_bf = act_own.astype(jnp.bfloat16)
    dots_own = jnp.sum(act_bf.astype(jnp.float32) * drive, axis=-1)
    grad_own = (gate_piece * drive * slope_own).astype(jnp.bfloat16)
    act_gated = (gate_piece * act_own).astype(jnp.bfloat16)
    back_own = jnp.einsum(
        "erf,ecf->erc", grad_own, up_weight, preferred_element_type=jnp.float32
    ).astype(jnp.bfloat16)
    back_sum = lax.psum_scatter(back_own, "space", scatter_dimension=1, tiled=True)
    row_dots = lax.psum_scatter(dots_own, "space", scatter_dimension=1, tiled=True)
    up_total = jnp.einsum("erc,erf->ecf", norm_piece, grad_own, preferred_element_type=jnp.float32)
    down_total = jnp.einsum("erc,erf->ecf", cot_piece, act_gated, preferred_element_type=jnp.float32)
    back_grad = back_sum.reshape(local_experts, group_count, CAP, channels)
    ret_grad, ret_dots = (
        lax.all_to_all(back_grad, "expert", split_axis=1, concat_axis=1, tiled=True),
        lax.all_to_all(
            row_dots.reshape(local_experts, group_count, CAP),
            "expert",
            split_axis=1,
            concat_axis=1,
            tiled=True,
        ),
    )
    choice_grad = (
        ret_grad.reshape(slot_total, channels)[destination]
        .astype(jnp.float32)
        .reshape(tokens, TOP, channels)
    )
    norm_grad = jnp.sum(choice_grad, axis=1)
    inner_mean = jnp.mean(norm_grad * norm_float, axis=-1, keepdims=True)
    residual_grad = (
        cot_rows.astype(jnp.float32) + (norm_grad - norm_float * inner_mean) / rms_value
    ).astype(jnp.bfloat16)
    choice_dots = ret_dots.reshape(slot_total)[destination].astype(jnp.float32).reshape(tokens, TOP)
    gate_drive = keep_float * choice_dots
    gate_mix = jnp.sum(gates_top * gate_drive, axis=-1, keepdims=True)
    gate_part = gates_top * (gate_drive - gate_mix)
    logit_gate = jnp.sum(jnp.where(one_hot, gate_part[:, :, None], 0.0), axis=1)
    expert_share = jnp.sum(jnp.where(one_hot, keep_float[:, :, None], 0.0), axis=(0, 1)) / (
        TOP * tokens
    )
    logit_max = jnp.max(router_logits, axis=-1, keepdims=True)
    logit_exp = jnp.exp(router_logits - logit_max)
    router_probs = logit_exp / jnp.sum(logit_exp, axis=-1, keepdims=True)
    share_mean = jnp.sum(router_probs * expert_share[None, :], axis=-1, keepdims=True)
    balance = EXPERTS * router_probs * (expert_share[None, :] - share_mean)
    logit_grad = (logit_gate + balance).reshape(1, win_side, map_width, EXPERTS)
    grad_map = residual_grad.reshape(win_side, map_width, channels)
    next_grad = from_behind(grad_map[:half_win], "space", -1)
    grad_shifted = jnp.concatenate([grad_map[half_win:], next_grad], axis=0)
    last_flags = jnp.reshape(space_index == space_count - 1, (1,))
    frame_grads = window_grads(qkv_shifted[:, None], grad_shifted[None], last_flags, HEADS)[:, 0]
    prev_rows = from_behind(frame_grads[:, half_win:], "space", 1)
    attn_grad = jnp.concatenate([prev_rows, frame_grads[:, :half_win]], axis=1)
    return (attn_grad[:, None], grad_map[None], up_total, down_total, logit_grad)


def solution(mesh):
    in_specs = (
        P(None, "expert", "space", None, None),
        P("expert", "space", None, None),
        P("expert", "space", None, None),
        P("expert", "space", None, None),
        P("expert", "space", None, None),
        P("expert", "space", None, None),
        P("expert", None, "space"),
        P("expert", None, "space"),
    )
    out_specs = (
        P(None, "expert", "space", None, None),
        P("expert", "space", None, None),
        P("expert", None, "space"),
        P("expert", None, "space"),
        P("expert", "space", None, None),
    )
    return jax.shard_map(
        per_device, mesh=mesh, in_specs=in_specs, out_specs=out_specs, check_vma=False
    )
```

```python
import functools
import math

import jax
import jax.numpy as jnp
from jax import lax
from jax.experimental import pallas as pl
from jax.experimental.pallas import tpu as pltpu
from jax.sharding import PartitionSpec as P

HEADS = 16
EXPERTS = 32
TOP = 2
CAP = 12


NORM_EPS = 1e-06
SCORE_MASK = -100.0


def from_behind(block, axis, distance):
    devices = range(lax.axis_size(axis))
    route = [((i - distance) % len(devices), i) for i in devices]
    return lax.ppermute(block, axis, route)


def gelu_pair(pre_act):
    activation, pullback = jax.vjp(jax.nn.gelu, pre_act)
    gelu_slope = pullback(jnp.ones_like(pre_act))[0]
    return (activation, gelu_slope)


def to_windows(tensor, head_count):
    blocks, win_side, map_width, channels = tensor.shape
    win_count = map_width // win_side
    head_dim = channels // head_count
    shaped = tensor.reshape(blocks, win_side, win_count, win_side, head_count, head_dim)
    shaped = shaped.transpose(0, 2, 4, 1, 3, 5)
    return shaped.reshape(blocks, win_count, head_count, win_side * win_side, head_dim)


def from_windows(tensor, win_side):
    blocks, win_count, head_count, win_area, head_dim = tensor.shape
    shaped = tensor.reshape(blocks, win_count, head_count, win_side, win_side, head_dim)
    shaped = shaped.transpose(0, 3, 1, 4, 2, 5)
    return shaped.reshape(blocks, win_side, win_count * win_side, head_count * head_dim)


def window_grads(frame_qkv, frame_grad, last_flags, head_count):
    win_side = frame_grad.shape[1]
    map_width = frame_grad.shape[2]
    half_win = win_side // 2
    head_dim = frame_grad.shape[3] // head_count
    inv_sqrt = head_dim ** (-0.5)
    rolled = jnp.roll(frame_qkv, -half_win, axis=3)
    grad_rolled = jnp.roll(frame_grad, -half_win, axis=2)
    query_win = to_windows(rolled[0], head_count)
    key_win = to_windows(rolled[1], head_count)
    value_win = to_windows(rolled[2], head_count)
    grad_win = to_windows(grad_rolled, head_count)
    row_pos = jnp.arange(win_side, dtype=jnp.int32)
    col_pos = jnp.arange(map_width, dtype=jnp.int32)
    row_label = jnp.where(last_flags[:, None], jnp.where(row_pos < half_win, 1, 2)[None, :], 0)
    col_label = jnp.where(
        col_pos >= map_width - win_side, jnp.where(col_pos < map_width - half_win, 1, 2), 0
    )
    region = 3 * row_label[:, :, None] + col_label[None, None, :]
    region = region.reshape(region.shape[0], win_side, map_width // win_side, win_side).transpose(
        0, 2, 1, 3
    )
    region = region.reshape(region.shape[0], region.shape[1], win_side * win_side)
    score_bias = jnp.where(region[:, :, :, None] != region[:, :, None, :], SCORE_MASK, 0.0)[
        :, :, None
    ]
    scores = (
        jnp.einsum("bnhqd,bnhkd->bnhqk", query_win, key_win, preferred_element_type=jnp.float32)
        * inv_sqrt
        + score_bias
    )
    row_max = jnp.max(scores, axis=-1, keepdims=True)
    exp_scores = jnp.exp(scores - row_max)
    attn_probs = exp_scores / jnp.sum(exp_scores, axis=-1, keepdims=True)
    weights_bf = attn_probs.astype(jnp.bfloat16)
    attn_out = jnp.einsum(
        "bnhqk,bnhkd->bnhqd", weights_bf, value_win, preferred_element_type=jnp.float32
    )
    row_delta = jnp.sum(grad_win.astype(jnp.float32) * attn_out, axis=-1, keepdims=True)
    prob_grad = jnp.einsum(
        "bnhqd,bnhkd->bnhqk", grad_win, value_win, preferred_element_type=jnp.float32
    )
    score_grad = (attn_probs * (prob_grad - row_delta)).astype(jnp.bfloat16)
    query_grad = (
        jnp.einsum("bnhqk,bnhkd->bnhqd", score_grad, key_win, preferred_element_type=jnp.float32)
        * inv_sqrt
    ).astype(jnp.bfloat16)
    key_grad = (
        jnp.einsum("bnhqk,bnhqd->bnhkd", score_grad, query_win, preferred_element_type=jnp.float32)
        * inv_sqrt
    ).astype(jnp.bfloat16)
    value_grad = jnp.einsum(
        "bnhqk,bnhqd->bnhkd", weights_bf, grad_win, preferred_element_type=jnp.float32
    ).astype(jnp.bfloat16)
    stacked = jnp.stack(
        [
            from_windows(query_grad, win_side),
            from_windows(key_grad, win_side),
            from_windows(value_grad, win_side),
        ]
    )
    return jnp.roll(stacked, half_win, axis=3)


def per_device_slots(
    attn_inputs, residual, logits, expert_ids, keep_mask, cotangent, up_weight, down_weight
):
    group_count = lax.axis_size("expert")
    local_experts = up_weight.shape[0]
    win_side = residual.shape[1]
    map_width = residual.shape[2]
    channels = residual.shape[3]
    tokens = win_side * map_width
    half_win = win_side // 2
    space_index = lax.axis_index("space")
    space_count = lax.axis_size("space")
    qkv_local = attn_inputs[:, 0]
    next_rows = from_behind(qkv_local[:, :half_win], "space", -1)
    qkv_shifted = jnp.concatenate([qkv_local[:, half_win:], next_rows], axis=1)
    resid_float = residual[0].reshape(tokens, channels).astype(jnp.float32)
    rms_value = jnp.sqrt(jnp.mean(resid_float * resid_float, axis=-1, keepdims=True) + NORM_EPS)
    norm_float = resid_float / rms_value
    normed = norm_float.astype(jnp.bfloat16)
    route_ids = expert_ids[0].reshape(tokens, TOP)
    keep_float = keep_mask[0].reshape(tokens, TOP).astype(jnp.float32)
    router_logits = logits[0].reshape(tokens, EXPERTS)
    expert_cols = jnp.arange(EXPERTS, dtype=jnp.int32)
    one_hot = route_ids[:, :, None] == expert_cols[None, None, :]
    chosen = jnp.sum(jnp.where(one_hot, router_logits[:, None, :], 0.0), axis=-1)
    chosen_max = jnp.max(chosen, axis=-1, keepdims=True)
    chosen_exp = jnp.exp(chosen - chosen_max)
    gates_top = chosen_exp / jnp.sum(chosen_exp, axis=-1, keepdims=True)
    gate_weight = gates_top * keep_float
    cot_rows = cotangent[0].reshape(tokens, channels)
    flat_hot = one_hot.reshape(tokens * TOP, EXPERTS).astype(jnp.int32)
    running = jnp.cumsum(flat_hot, axis=0) - flat_hot
    slot_index = jnp.sum(running * flat_hot, axis=-1)
    flat_ids = route_ids.reshape(-1)
    destination = (
        flat_ids % local_experts * group_count + flat_ids // local_experts
    ) * CAP + slot_index
    slot_total = local_experts * group_count * CAP
    choice_norm = jnp.broadcast_to(normed[:, None, :], (tokens, TOP, channels)).reshape(
        tokens * TOP, channels
    )
    choice_cot = jnp.broadcast_to(cot_rows[:, None, :], (tokens, TOP, channels)).reshape(
        tokens * TOP, channels
    )
    send_norm = (
        jnp.zeros((slot_total, channels), jnp.bfloat16)
        .at[destination]
        .set(choice_norm)
        .reshape(local_experts, group_count, CAP, channels)
    )
    send_cot = (
        jnp.zeros((slot_total, channels), jnp.bfloat16)
        .at[destination]
        .set(choice_cot)
        .reshape(local_experts, group_count, CAP, channels)
    )
    send_gate = (
        jnp.zeros((slot_total,), jnp.float32)
        .at[destination]
        .set(gate_weight.reshape(tokens * TOP))
        .reshape(local_experts, group_count, CAP)
    )
    recv_norm, recv_cot, recv_gate = (
        lax.all_to_all(send_norm, "expert", split_axis=1, concat_axis=1, tiled=True),
        lax.all_to_all(send_cot, "expert", split_axis=1, concat_axis=1, tiled=True),
        lax.all_to_all(send_gate, "expert", split_axis=1, concat_axis=1, tiled=True),
    )
    expert_rows = group_count * CAP
    in_rows = recv_norm.reshape(local_experts, expert_rows, channels)
    cot_in = recv_cot.reshape(local_experts, expert_rows, channels)
    gate_in = recv_gate.reshape(local_experts, expert_rows)
    norm_piece = lax.all_gather(in_rows, "space", axis=1, tiled=True)
    cot_piece = lax.all_gather(cot_in, "space", axis=1, tiled=True)
    gate_piece = lax.all_gather(gate_in, "space", axis=1, tiled=True)[:, :, None]
    pre_own = jnp.einsum("erc,ecf->erf", norm_piece, up_weight, preferred_element_type=jnp.float32)
    act_own, slope_own = gelu_pair(pre_own)
    drive = jnp.einsum("erc,ecf->erf", cot_piece, down_weight, preferred_element_type=jnp.float32)
    act_bf = act_own.astype(jnp.bfloat16)
    dots_own = jnp.sum(act_bf.astype(jnp.float32) * drive, axis=-1)
    grad_own = (gate_piece * drive * slope_own).astype(jnp.bfloat16)
    act_gated = (gate_piece * act_own).astype(jnp.bfloat16)
    back_own = jnp.einsum(
        "erf,ecf->erc", grad_own, up_weight, preferred_element_type=jnp.float32
    ).astype(jnp.bfloat16)
    back_sum = lax.psum_scatter(back_own, "space", scatter_dimension=1, tiled=True)
    row_dots = lax.psum_scatter(dots_own, "space", scatter_dimension=1, tiled=True)
    up_total = jnp.einsum("erc,erf->ecf", norm_piece, grad_own, preferred_element_type=jnp.float32)
    down_total = jnp.einsum("erc,erf->ecf", cot_piece, act_gated, preferred_element_type=jnp.float32)
    back_grad = back_sum.reshape(local_experts, group_count, CAP, channels)
    ret_grad, ret_dots = (
        lax.all_to_all(back_grad, "expert", split_axis=1, concat_axis=1, tiled=True),
        lax.all_to_all(
            row_dots.reshape(local_experts, group_count, CAP),
            "expert",
            split_axis=1,
            concat_axis=1,
            tiled=True,
        ),
    )
    choice_grad = (
        ret_grad.reshape(slot_total, channels)[destination]
        .astype(jnp.float32)
        .reshape(tokens, TOP, channels)
    )
    norm_grad = jnp.sum(choice_grad, axis=1)
    inner_mean = jnp.mean(norm_grad * norm_float, axis=-1, keepdims=True)
    residual_grad = (
        cot_rows.astype(jnp.float32) + (norm_grad - norm_float * inner_mean) / rms_value
    ).astype(jnp.bfloat16)
    choice_dots = ret_dots.reshape(slot_total)[destination].astype(jnp.float32).reshape(tokens, TOP)
    gate_drive = keep_float * choice_dots
    gate_mix = jnp.sum(gates_top * gate_drive, axis=-1, keepdims=True)
    gate_part = gates_top * (gate_drive - gate_mix)
    logit_gate = jnp.sum(jnp.where(one_hot, gate_part[:, :, None], 0.0), axis=1)
    expert_share = jnp.sum(jnp.where(one_hot, keep_float[:, :, None], 0.0), axis=(0, 1)) / (
        TOP * tokens
    )
    logit_max = jnp.max(router_logits, axis=-1, keepdims=True)
    logit_exp = jnp.exp(router_logits - logit_max)
    router_probs = logit_exp / jnp.sum(logit_exp, axis=-1, keepdims=True)
    share_mean = jnp.sum(router_probs * expert_share[None, :], axis=-1, keepdims=True)
    balance = EXPERTS * router_probs * (expert_share[None, :] - share_mean)
    logit_grad = (logit_gate + balance).reshape(1, win_side, map_width, EXPERTS)
    grad_map = residual_grad.reshape(win_side, map_width, channels)
    next_grad = from_behind(grad_map[:half_win], "space", -1)
    grad_shifted = jnp.concatenate([grad_map[half_win:], next_grad], axis=0)
    last_flags = jnp.reshape(space_index == space_count - 1, (1,))
    frame_grads = window_grads(qkv_shifted[:, None], grad_shifted[None], last_flags, HEADS)[:, 0]
    prev_rows = from_behind(frame_grads[:, half_win:], "space", 1)
    attn_grad = jnp.concatenate([prev_rows, frame_grads[:, :half_win]], axis=1)
    return (attn_grad[:, None], grad_map[None], up_total, down_total, logit_grad)


META = 8
PAD = 16
GELU_C = math.sqrt(2.0 / math.pi)
GELU_A = 0.044715


def iota(shape, dim):
    return lax.broadcasted_iota(jnp.int32, shape, dim)


def dot(a, b, ca, cb):
    return lax.dot_general(a, b, (((ca,), (cb,)), ((), ())), preferred_element_type=jnp.float32)


def to_lanes(column):
    n = column.shape[0]
    return jnp.sum(jnp.where(iota((n, n), 0) == iota((n, n), 1), column, 0.0), axis=0, keepdims=True)


def to_rows(row):
    n = row.shape[1]
    return jnp.sum(jnp.where(iota((n, n), 0) == iota((n, n), 1), row, 0.0), axis=1, keepdims=True)


def stack_rows(rows):
    out = jnp.zeros((META, rows[0].shape[1]), jnp.float32)
    sub = iota(out.shape, 0)
    for k, row in enumerate(rows):
        out = jnp.where(sub == k, row, out)
    return out


def split_hi_lo(x):
    hi = x.astype(jnp.bfloat16).astype(jnp.float32)
    return hi, x - hi


def routing(logits, ids, keep):
    tokens, experts = logits.shape
    cols = iota((tokens, experts), 1)
    hot = [cols == ids[:, k : k + 1] for k in range(TOP)]
    z = [jnp.sum(jnp.where(h, logits, 0.0), axis=-1, keepdims=True) for h in hot]
    top = jnp.maximum(z[0], z[1])
    ex = [jnp.exp(v - top) for v in z]
    total = ex[0] + ex[1]
    gates = [v / total for v in ex]
    keeps = [keep[:, k : k + 1].astype(jnp.float32) for k in range(TOP)]
    return hot, gates, keeps


def prep_kernel(res_ref, log_ref, ids_ref, keep_ref, cot_ref, out_ref):
    tokens, channels = res_ref.shape
    res = res_ref[...].astype(jnp.float32)
    rms = jnp.sqrt(jnp.mean(res * res, axis=-1, keepdims=True) + NORM_EPS)
    out_ref[0, :tokens, :] = (res / rms).astype(jnp.bfloat16)
    out_ref[1, :tokens, :] = cot_ref[...]
    ids = ids_ref[...]
    hot, gates, keeps = routing(log_ref[...], ids, keep_ref[...])
    both = jnp.where(hot[0] | hot[1], 1.0, 0.0).astype(jnp.bfloat16)
    earlier = jnp.where(iota((tokens, tokens), 1) < iota((tokens, tokens), 0), 1.0, 0.0)
    count = dot(earlier.astype(jnp.bfloat16), both, 1, 0)
    where, weight = [], []
    for k in range(TOP):
        slot = jnp.sum(jnp.where(hot[k], count, 0.0), axis=-1, keepdims=True)
        where += [ids[:, k : k + 1].astype(jnp.float32), slot]
        weight += split_hi_lo(gates[k] * keeps[k])
    for side, cols in ((0, where), (1, weight)):
        out_ref[side, tokens:, :] = jnp.zeros((META, channels), jnp.bfloat16)
        rows = stack_rows([to_lanes(c) for c in cols])
        out_ref[side, tokens:, :tokens] = rows.astype(jnp.bfloat16)


def ffn_kernel(chunks, tokens, base_ref, *refs):
    tok_refs = refs[: 2 * chunks]
    up_ref, down_ref = refs[2 * chunks : 2 * chunks + 2]
    mine_ref, part_ref, x_ref, pg_ref, ag_ref = refs[2 * chunks + 2 : 2 * chunks + 7]
    xs, gs, ds, rs = refs[2 * chunks + 7 :]
    rows = xs.shape[1]
    channels = up_ref.shape[1]
    half = channels // 2
    step = pl.program_id(0)
    side = [0, 2, 1, 3]
    strips = []
    for c in range(chunks):
        for who in range(2):
            for i in range(4):
                strips.append((tok_refs[2 * c + who], i, 4 + side[i], who, c * 4 + i))

    def choices(ref, n_at):
        meta = ref[n_at, tokens:, :].astype(jnp.float32)[:, :tokens]
        base = base_ref[0].astype(jnp.float32)
        line = iota((rows, tokens), 0).astype(jnp.float32)
        return [
            line == (meta[2 * k : 2 * k + 1] - base) * PAD + meta[2 * k + 1 : 2 * k + 2]
            for k in range(TOP)
        ]

    @pl.when(step == 0)
    def _():
        for i, (ref, n_at, c_at, _, _) in enumerate(strips):
            picks = choices(ref, n_at)
            pick = jnp.where(picks[0] | picks[1], 1.0, 0.0).astype(jnp.bfloat16)
            gate = ref[c_at, tokens:, :].astype(jnp.float32)[:, :tokens]
            xs[i, :, :channels] = dot(pick, ref[n_at, :tokens, :], 1, 0).astype(jnp.bfloat16)
            xs[i, :, channels:] = dot(pick, ref[c_at, :tokens, :], 1, 0).astype(jnp.bfloat16)
            weight = sum(
                jnp.where(picks[k], gate[2 * k : 2 * k + 1] + gate[2 * k + 1 : 2 * k + 2], 0.0)
                for k in range(TOP)
            )
            gs[i] = jnp.sum(weight, axis=1, keepdims=True)

    count = len(strips) * PAD
    at = pl.ds(pl.multiple_of(step * PAD, PAD), PAD)
    x = xs[:, at, :].reshape(count, 2 * channels)
    g = gs[:, at, :].reshape(count, 1)
    x_ref[0] = x
    pre = dot(x[:, :channels], up_ref[0], 1, 0)
    drive = dot(x[:, channels:], down_ref[0], 1, 0)
    sq = pre * pre
    t = jnp.tanh(GELU_C * (pre + GELU_A * (sq * pre)))
    act = 0.5 * pre * (1.0 + t)
    slope = 0.5 * (1.0 + t) + 0.5 * pre * (1.0 - t * t) * (GELU_C * (1.0 + 3.0 * GELU_A * sq))
    dots = jnp.sum(act.astype(jnp.bfloat16).astype(jnp.float32) * drive, axis=1, keepdims=True)
    ds[:, at, :] = dots.reshape(len(strips), PAD, 1)
    ag_ref[0] = (g * act).astype(jnp.bfloat16)
    pg = (g * drive * slope).astype(jnp.bfloat16)
    pg_ref[0] = pg
    back = dot(pg, up_ref[0], 1, 1).astype(jnp.bfloat16)
    rs[:, at, :] = back.reshape(len(strips), PAD, channels)

    @pl.when(step == pl.num_programs(0) - 1)
    def _():
        for i, (ref, n_at, _, who, to) in enumerate(strips):
            picks = choices(ref, n_at)
            pick = jnp.where(picks[0] | picks[1], 1.0, 0.0).astype(jnp.bfloat16)
            grad = dot(pick, rs[i], 0, 0).astype(jnp.bfloat16)
            d = [jnp.sum(jnp.where(p, ds[i], 0.0), axis=0, keepdims=True) for p in picks]
            d = [split_hi_lo(v) for v in d]
            out = mine_ref if who == 0 else part_ref
            for h in range(2):
                out[h, to, :tokens, :] = grad[:, h * half : (h + 1) * half]
                out[h, to, tokens:, :] = jnp.zeros((META, half), jnp.bfloat16)
            rows_d = stack_rows([d[0][0], d[1][0], d[0][1], d[1][1]])
            out[0, to, tokens:, :tokens] = rows_d.astype(jnp.bfloat16)


def run_ffn(base, mine, part, up, down, tokens):
    chunks = len(mine)
    experts, channels, hidden = up.shape
    strips = 8 * chunks
    count = strips * PAD
    toks = [a for pair in zip(mine, part) for a in pair]
    half = channels // 2
    whole = lambda shape: pl.BlockSpec(shape, lambda j: (0,) * len(shape))
    each = lambda shape: pl.BlockSpec((1,) + shape, lambda j: (j,) + (0,) * len(shape))
    out_t = (2, 4 * chunks, tokens + META, half)
    bf = jnp.bfloat16
    flops = 2 * experts * count * channels * hidden * 3
    return pl.pallas_call(
        functools.partial(ffn_kernel, chunks, tokens),
        grid=(experts,),
        out_shape=[
            jax.ShapeDtypeStruct(out_t, bf),
            jax.ShapeDtypeStruct(out_t, bf),
            jax.ShapeDtypeStruct((experts, count, 2 * channels), bf),
            jax.ShapeDtypeStruct((experts, count, hidden), bf),
            jax.ShapeDtypeStruct((experts, count, hidden), bf),
        ],
        in_specs=[pl.BlockSpec(memory_space=pltpu.SMEM)]
        + [whole(a.shape) for a in toks]
        + [each((channels, hidden))] * 2,
        out_specs=[
            whole(out_t),
            whole(out_t),
            each((count, 2 * channels)),
            each((count, hidden)),
            each((count, hidden)),
        ],
        scratch_shapes=[
            pltpu.VMEM((strips, experts * PAD, 2 * channels), bf),
            pltpu.VMEM((strips, experts * PAD, 1), jnp.float32),
            pltpu.VMEM((strips, experts * PAD, 1), jnp.float32),
            pltpu.VMEM((strips, experts * PAD, channels), bf),
        ],
        compiler_params=pltpu.CompilerParams(dimension_semantics=("arbitrary",)),
        cost_estimate=pl.CostEstimate(
            flops=2 * flops, bytes_accessed=2 * up.size * 2 + count * 4096 * experts, transcendentals=0
        ),
        name="ffn",
    )(base, *toks, up, down)


def wgrad_kernel(n, *refs):
    xs, pgs, ags = refs[:n], refs[n : 2 * n], refs[2 * n : 3 * n]
    up_ref, down_ref = refs[3 * n :]
    channels = up_ref.shape[1]
    up = down = 0.0
    for x, pg, ag in zip(xs, pgs, ags):
        up = up + dot(x[0, :, :channels], pg[0], 0, 0)
        down = down + dot(x[0, :, channels:], ag[0], 0, 0)
    up_ref[0] = up
    down_ref[0] = down


def run_wgrad(xs, pgs, ags):
    experts, _, two = xs[0].shape
    hidden = pgs[0].shape[2]
    each = lambda shape: pl.BlockSpec((1,) + shape[1:], lambda j: (j, 0, 0))
    out = (experts, two // 2, hidden)
    ops = list(xs) + list(pgs) + list(ags)
    rows = sum(x.shape[1] for x in xs)
    return pl.pallas_call(
        functools.partial(wgrad_kernel, len(xs)),
        grid=(experts,),
        out_shape=[jax.ShapeDtypeStruct(out, jnp.float32)] * 2,
        in_specs=[each(a.shape) for a in ops],
        out_specs=[each(out)] * 2,
        compiler_params=pltpu.CompilerParams(dimension_semantics=("arbitrary",)),
        cost_estimate=pl.CostEstimate(
            flops=4 * experts * rows * two * hidden,
            bytes_accessed=sum(a.size * 2 for a in ops) + 8 * experts * two * hidden // 2,
            transcendentals=0,
        ),
        name="wgrad",
    )(*ops)


def add_blocks(a, b, tokens):
    s = a.astype(jnp.float32) + b.astype(jnp.float32)
    return s[:tokens].astype(jnp.bfloat16), meta_sum(s[tokens:]).astype(jnp.bfloat16)


def meta_sum(s):
    total = s + pltpu.roll(s, META - TOP, 0)
    hi, lo = split_hi_lo(total)
    sub = iota(s.shape, 0)
    return jnp.where(sub < TOP, hi, jnp.where(sub < 2 * TOP, pltpu.roll(lo, TOP, 0), 0.0))


def put(ref, at, a, b, tokens):
    body, meta = add_blocks(a, b, tokens)
    ref[at, :tokens, :] = body
    ref[at, tokens:, :] = meta


def core_sum_kernel(chunks, tokens, mine_ref, got_ref, k1_ref, s1_ref, k2_ref, s2_ref):
    for c in range(chunks):
        for y in range(2):
            for x in range(2):
                i = c * 4 + y * 2 + x
                put((k1_ref, s1_ref)[x], c * 2 + y, mine_ref[0, i], got_ref[0, i], tokens)
                put((k2_ref, s2_ref)[y], c * 2 + x, mine_ref[1, i], got_ref[1, i], tokens)


def pair_sum_kernel(chunks, tokens, a1, b1, a2, b2, k1_ref, s1_ref, k2_ref, s2_ref):
    for c in range(chunks):
        for u in range(2):
            i = c * 2 + u
            put((k1_ref, s1_ref)[u], c, a1[i], b1[i], tokens)
            put((k2_ref, s2_ref)[u], c, a2[i], b2[i], tokens)


def last_sum_kernel(tokens, a1, b1, a2, b2, *outs):
    for c, ref in enumerate(outs):
        put(ref, 0, a1[c], b1[c], tokens)
        put(ref, 1, a2[c], b2[c], tokens)


def vmem_call(kernel, outs, *ops, name):
    full = pl.BlockSpec(memory_space=pltpu.VMEM)
    size = sum(a.size * a.dtype.itemsize for a in list(ops) + list(outs))
    return pl.pallas_call(
        kernel,
        out_shape=outs,
        in_specs=[full] * len(ops),
        out_specs=[full] * len(outs),
        cost_estimate=pl.CostEstimate(flops=size, bytes_accessed=size, transcendentals=0),
        name=name,
    )(*ops)


def final_kernel(n, res_ref, log_ref, ids_ref, keep_ref, cot_ref, *refs):
    parts = refs[:n]
    up_ref, low_ref, log_out = refs[n:]
    tokens, channels = res_ref.shape
    res = res_ref[...].astype(jnp.float32)
    rms = jnp.sqrt(jnp.mean(res * res, axis=-1, keepdims=True) + NORM_EPS)
    nf = res / rms
    halves = [sum(p[h].astype(jnp.float32) for p in parts) for h in range(2)]
    grad = jnp.concatenate([h[:tokens] for h in halves], axis=1)
    inner = jnp.mean(grad * nf, axis=-1, keepdims=True)
    out = cot_ref[...].astype(jnp.float32) + (grad - nf * inner) / rms
    mid = tokens // 2
    up_ref[...] = out[:mid].astype(jnp.bfloat16)
    low_ref[...] = out[mid:].astype(jnp.bfloat16)
    meta = halves[0][tokens:]
    total = (meta + pltpu.roll(meta, META - TOP, 0))[:, :tokens]
    logits = log_ref[...]
    experts = logits.shape[1]
    hot, gates, keeps = routing(logits, ids_ref[...], keep_ref[...])
    drive = [keeps[k] * to_rows(total[k : k + 1]).astype(jnp.bfloat16).astype(jnp.float32) for k in range(TOP)]
    mix = gates[0] * drive[0] + gates[1] * drive[1]
    part = sum(jnp.where(hot[k], gates[k] * (drive[k] - mix), 0.0) for k in range(TOP))
    share = sum(
        jnp.sum(jnp.where(hot[k], keeps[k], 0.0), axis=0, keepdims=True) for k in range(TOP)
    ) / (TOP * tokens)
    top = jnp.max(logits, axis=-1, keepdims=True)
    ex = jnp.exp(logits - top)
    probs = ex / jnp.sum(ex, axis=-1, keepdims=True)
    mean = jnp.sum(probs * share, axis=-1, keepdims=True)
    log_out[...] = part + experts * probs * (share - mean)


def attn_kernel(heads, q_ref, k_ref, v_ref, g1_ref, g2_ref, kl_ref, ql_ref, out_ref):
    area, width = q_ref.shape[1:]
    mid = area // 2
    dim = width // heads
    inv = dim**-0.5
    lane = iota((area, width), 1) // dim
    q, k, v = q_ref[0], k_ref[0], v_ref[0]
    g = jnp.concatenate(
        [g1_ref[0].astype(jnp.float32), g2_ref[0].astype(jnp.float32)], axis=0
    ).astype(jnp.bfloat16)
    masks = [jnp.where(lane == h, 1.0, 0.0) for h in range(heads)]
    spread = lambda a: jnp.concatenate([a * m.astype(jnp.bfloat16) for m in masks], axis=0)
    qs, gsp = spread(q), spread(g)
    scores = dot(k, qs, 1, 1) * inv + jnp.where(kl_ref[0] != ql_ref[0], SCORE_MASK, 0.0)
    ex = jnp.exp(scores - jnp.max(scores, axis=0, keepdims=True))
    probs = ex * (1.0 / jnp.sum(ex, axis=0, keepdims=True))
    weights = probs.astype(jnp.bfloat16)
    pgrad = dot(v, gsp, 1, 1)
    delta = jnp.sum(weights.astype(jnp.float32) * pgrad, axis=0, keepdims=True)
    sgrad = (probs * (pgrad - delta)).astype(jnp.bfloat16)
    dk = dot(sgrad, qs, 1, 0) * inv
    dv = dot(weights, gsp, 1, 0)
    wide = dot(sgrad, k, 0, 0)
    dq = sum(wide[h * area : (h + 1) * area] * masks[h] for h in range(heads)) * inv
    first = pl.program_id(0) == 0
    for n, a in enumerate((dq, dk, dv)):
        out_ref[n, 0] = jnp.where(first, a[:mid], a[mid:]).astype(jnp.bfloat16)


def run_attention(q, k, v, g1, g2, klab, qlab, groups):
    _, area, channels = q.shape
    width = channels // groups
    heads = HEADS // groups
    mid = area // 2
    win = lambda rows: pl.BlockSpec((1, rows, width), lambda w, g: (w, 0, g))
    return pl.pallas_call(
        functools.partial(attn_kernel, heads),
        grid=(2, groups),
        out_shape=jax.ShapeDtypeStruct((3, 2, mid, channels), jnp.bfloat16),
        in_specs=[win(area)] * 3
        + [win(mid)] * 2
        + [
            pl.BlockSpec((1, area, 1), lambda w, g: (w, 0, 0)),
            pl.BlockSpec((1, 1, heads * area), lambda w, g: (w, 0, 0)),
        ],
        out_specs=pl.BlockSpec((3, 1, mid, width), lambda w, g: (0, 1 - w, 0, g)),
        compiler_params=pltpu.CompilerParams(dimension_semantics=("arbitrary", "arbitrary")),
        cost_estimate=pl.CostEstimate(
            flops=20 * area * area * channels * heads, bytes_accessed=16 * q.size, transcendentals=0
        ),
        name="attn",
    )(q, k, v, g1, g2, klab, qlab)


FFN_GROUPS = ((0, 1), (2, 3))


def per_device_tokens(
    attn_inputs, residual, logits, expert_ids, keep_mask, cotangent, up_weight, down_weight
):
    n_exp, n_space = lax.axis_size("expert"), lax.axis_size("space")
    local = up_weight.shape[0]
    win_side, map_width, channels = residual.shape[1:]
    tokens = win_side * map_width
    mid = tokens // 2
    deep = n_space // 2

    def send(block, dz=0, dx=0, dy=0, dc=0):
        pairs = []
        for e in range(n_exp):
            for s in range(n_space):
                y, c, z, x = e // 2, e % 2, s // 2, s % 2
                to_e = (y + dy) % (n_exp // 2) * 2 + (c + dc) % 2
                to_s = (z + dz) % deep * 2 + (x + dx) % 2
                pairs.append((e * n_space + s, to_e * n_space + to_s))
        return lax.ppermute(block, ("expert", "space"), pairs)

    res = residual[0].reshape(tokens, channels)
    cot = cotangent[0].reshape(tokens, channels)
    log = logits[0].reshape(tokens, EXPERTS)
    ids = expert_ids[0].reshape(tokens, TOP)
    keep = keep_mask[0].reshape(tokens, TOP)
    bf = jnp.bfloat16
    deal = jax.ShapeDtypeStruct
    block = vmem_call(
        prep_kernel,
        [deal((2, tokens + META, channels), bf)],
        res, log, ids, keep, cot,
        name="prep",
    )[0]
    mine, part = [], []
    moved = [block] + [send(block, dz=d) for d in range(1, deep)]
    for d in range(deep):
        n0, c0 = moved[d][:1], moved[d][1:]
        n1 = send(n0, dx=1)
        c1 = send(c0, dy=1)
        n01 = jnp.concatenate([n0, n1])
        c01 = jnp.concatenate([c0, c1])
        n23 = send(n01, dy=1)
        c23 = send(c01, dx=1)
        full = jnp.concatenate([n01, n23, c01, c23])
        mine.append(full)
        part.append(send(full, dc=1))

    qkv = attn_inputs[:, 0].reshape(3, tokens, channels)
    upper, lower = qkv[:, :mid], qkv[:, mid:]
    after = from_behind(upper, "space", -1)
    before = from_behind(lower, "space", 1)
    frame = jnp.stack(
        [jnp.concatenate([lower, after], axis=1), jnp.concatenate([before, upper], axis=1)], axis=1
    )

    base = jnp.reshape(lax.axis_index("expert") * local, (1,)).astype(jnp.int32)
    xs, pgs, ags, parts = [], [], [], []
    rows = tokens + META
    half = channels // 2
    for group in FFN_GROUPS:
        n = len(group)
        t_mine, t_part, x, pg, ag = run_ffn(
            base, [mine[d] for d in group], [part[d] for d in group], up_weight, down_weight, tokens
        )
        xs.append(x)
        pgs.append(pg)
        ags.append(ag)
        got = send(t_part, dc=1)
        two = deal((2 * n, rows, half), bf)
        k1, s1, k2, s2 = vmem_call(
            functools.partial(core_sum_kernel, n, tokens), [two] * 4, t_mine, got, name="csum"
        )
        r1, r2 = send(s1, dx=1), send(s2, dy=1)
        one = deal((n, rows, half), bf)
        k1, s1, k2, s2 = vmem_call(
            functools.partial(pair_sum_kernel, n, tokens), [one] * 4, k1, r1, k2, r2, name="psum"
        )
        r1, r2 = send(s1, dy=1), send(s2, dx=1)
        done = vmem_call(
            functools.partial(last_sum_kernel, tokens),
            [deal((2, rows, half), bf)] * n,
            k1, r1, k2, r2,
            name="lsum",
        )
        for d, w in zip(group, done):
            parts.append(w if d == 0 else send(w, dz=-d))
    up_total, down_total = run_wgrad(xs, pgs, ags)

    g_up, g_low, logit_grad = vmem_call(
        functools.partial(final_kernel, deep),
        [deal((mid, channels), bf)] * 2 + [deal((tokens, EXPERTS), jnp.float32)],
        res, log, ids, keep, cot, *parts,
        name="final",
    )
    g_after = from_behind(g_up, "space", -1)
    g_before = from_behind(g_low, "space", 1)
    first = jnp.stack([g_low, g_before])
    second = jnp.stack([g_after, g_up])
    space = lax.axis_index("space")
    last = jnp.stack([space == n_space - 1, space == 0]).astype(jnp.float32)
    at = jnp.arange(tokens, dtype=jnp.int32)
    late_col = (at % map_width >= map_width - win_side // 2).astype(jnp.float32)
    late_row = (at >= mid).astype(jnp.float32)
    label = late_col[None] + 2.0 * last[:, None] * late_row[None]
    groups = 2
    grads = run_attention(
        frame[0], frame[1], frame[2], first, second,
        label[:, :, None], jnp.tile(label, (1, HEADS // groups))[:, None], groups,
    )
    attn_grad = grads.reshape(3, 1, win_side, map_width, channels)
    residual_grad = jnp.concatenate([g_up, g_low]).reshape(1, win_side, map_width, channels)
    return (
        attn_grad,
        residual_grad,
        up_total,
        down_total,
        logit_grad.reshape(1, win_side, map_width, EXPERTS),
    )


def solution(mesh):
    n_exp, n_space = mesh.shape["expert"], mesh.shape["space"]
    local = EXPERTS // n_exp

    def per_device(attn_inputs, residual, *rest):
        win_side, map_width = residual.shape[1:3]
        gather_tokens = (
            win_side * map_width <= 2 * local * CAP
            and map_width == win_side
            and n_exp == 4
            and n_space % 2 == 0
        )
        plan = per_device_tokens if gather_tokens else per_device_slots
        return plan(attn_inputs, residual, *rest)

    in_specs = (
        P(None, "expert", "space", None, None),
        P("expert", "space", None, None),
        P("expert", "space", None, None),
        P("expert", "space", None, None),
        P("expert", "space", None, None),
        P("expert", "space", None, None),
        P("expert", None, "space"),
        P("expert", None, "space"),
    )
    out_specs = (
        P(None, "expert", "space", None, None),
        P("expert", "space", None, None),
        P("expert", None, "space"),
        P("expert", None, "space"),
        P("expert", "space", None, None),
    )
    return jax.shard_map(
        per_device, mesh=mesh, in_specs=in_specs, out_specs=out_specs, check_vma=False
    )
```

```python
import functools
import math

import jax
import jax.numpy as jnp
from jax import lax
from jax.experimental import pallas as pl
from jax.experimental.pallas import tpu as pltpu
from jax.sharding import PartitionSpec as P


HEADS = 16
EXPERTS = 32
TOP = 2
CAP = 12
TOKENS = 144


NORM_EPS = 1e-06
SCORE_MASK = -100.0


def from_behind(block, axis, distance):
    devices = range(lax.axis_size(axis))
    route = [((i - distance) % len(devices), i) for i in devices]
    return lax.ppermute(block, axis, route)


def gelu_pair(pre_act):
    activation, pullback = jax.vjp(jax.nn.gelu, pre_act)
    gelu_slope = pullback(jnp.ones_like(pre_act))[0]
    return (activation, gelu_slope)


def to_windows(tensor, head_count):
    blocks, win_side, map_width, channels = tensor.shape
    win_count = map_width // win_side
    head_dim = channels // head_count
    shaped = tensor.reshape(blocks, win_side, win_count, win_side, head_count, head_dim)
    shaped = shaped.transpose(0, 2, 4, 1, 3, 5)
    return shaped.reshape(blocks, win_count, head_count, win_side * win_side, head_dim)


def from_windows(tensor, win_side):
    blocks, win_count, head_count, _, head_dim = tensor.shape
    shaped = tensor.reshape(blocks, win_count, head_count, win_side, win_side, head_dim)
    shaped = shaped.transpose(0, 3, 1, 4, 2, 5)
    return shaped.reshape(blocks, win_side, win_count * win_side, head_count * head_dim)


def window_grads(frame_qkv, frame_grad, last_flags, head_count):
    win_side = frame_grad.shape[1]
    map_width = frame_grad.shape[2]
    half_win = win_side // 2
    head_dim = frame_grad.shape[3] // head_count
    inv_sqrt = head_dim ** (-0.5)
    rolled = jnp.roll(frame_qkv, -half_win, axis=3)
    grad_rolled = jnp.roll(frame_grad, -half_win, axis=2)
    query_win = to_windows(rolled[0], head_count)
    key_win = to_windows(rolled[1], head_count)
    value_win = to_windows(rolled[2], head_count)
    grad_win = to_windows(grad_rolled, head_count)
    row_pos = jnp.arange(win_side, dtype=jnp.int32)
    col_pos = jnp.arange(map_width, dtype=jnp.int32)
    row_label = jnp.where(last_flags[:, None], jnp.where(row_pos < half_win, 1, 2)[None, :], 0)
    col_label = jnp.where(
        col_pos >= map_width - win_side, jnp.where(col_pos < map_width - half_win, 1, 2), 0
    )
    region = 3 * row_label[:, :, None] + col_label[None, None, :]
    region = region.reshape(region.shape[0], win_side, map_width // win_side, win_side).transpose(
        0, 2, 1, 3
    )
    region = region.reshape(region.shape[0], region.shape[1], win_side * win_side)
    score_bias = jnp.where(region[:, :, :, None] != region[:, :, None, :], SCORE_MASK, 0.0)[
        :, :, None
    ]
    scores = (
        jnp.einsum("bnhqd,bnhkd->bnhqk", query_win, key_win, preferred_element_type=jnp.float32)
        * inv_sqrt
        + score_bias
    )
    row_max = jnp.max(scores, axis=-1, keepdims=True)
    exp_scores = jnp.exp(scores - row_max)
    attn_probs = exp_scores / jnp.sum(exp_scores, axis=-1, keepdims=True)
    weights_bf = attn_probs.astype(jnp.bfloat16)
    attn_out = jnp.einsum(
        "bnhqk,bnhkd->bnhqd", weights_bf, value_win, preferred_element_type=jnp.float32
    )
    row_delta = jnp.sum(grad_win.astype(jnp.float32) * attn_out, axis=-1, keepdims=True)
    prob_grad = jnp.einsum(
        "bnhqd,bnhkd->bnhqk", grad_win, value_win, preferred_element_type=jnp.float32
    )
    score_grad = (attn_probs * (prob_grad - row_delta)).astype(jnp.bfloat16)
    query_grad = (
        jnp.einsum("bnhqk,bnhkd->bnhqd", score_grad, key_win, preferred_element_type=jnp.float32)
        * inv_sqrt
    ).astype(jnp.bfloat16)
    key_grad = (
        jnp.einsum("bnhqk,bnhqd->bnhkd", score_grad, query_win, preferred_element_type=jnp.float32)
        * inv_sqrt
    ).astype(jnp.bfloat16)
    value_grad = jnp.einsum(
        "bnhqk,bnhqd->bnhkd", weights_bf, grad_win, preferred_element_type=jnp.float32
    ).astype(jnp.bfloat16)
    stacked = jnp.stack(
        [
            from_windows(query_grad, win_side),
            from_windows(key_grad, win_side),
            from_windows(value_grad, win_side),
        ]
    )
    return jnp.roll(stacked, half_win, axis=3)


def per_device_slots(
    attn_inputs, residual, logits, expert_ids, keep_mask, cotangent, up_weight, down_weight
):
    group_count = lax.axis_size("expert")
    local_experts = up_weight.shape[0]
    win_side = residual.shape[1]
    map_width = residual.shape[2]
    channels = residual.shape[3]
    tokens = win_side * map_width
    half_win = win_side // 2
    space_index = lax.axis_index("space")
    space_count = lax.axis_size("space")
    qkv_local = attn_inputs[:, 0]
    next_rows = from_behind(qkv_local[:, :half_win], "space", -1)
    qkv_shifted = jnp.concatenate([qkv_local[:, half_win:], next_rows], axis=1)
    resid_float = residual[0].reshape(tokens, channels).astype(jnp.float32)
    rms_value = jnp.sqrt(jnp.mean(resid_float * resid_float, axis=-1, keepdims=True) + NORM_EPS)
    norm_float = resid_float / rms_value
    normed = norm_float.astype(jnp.bfloat16)
    route_ids = expert_ids[0].reshape(tokens, TOP)
    keep_float = keep_mask[0].reshape(tokens, TOP).astype(jnp.float32)
    router_logits = logits[0].reshape(tokens, EXPERTS)
    expert_cols = jnp.arange(EXPERTS, dtype=jnp.int32)
    one_hot = route_ids[:, :, None] == expert_cols[None, None, :]
    chosen = jnp.sum(jnp.where(one_hot, router_logits[:, None, :], 0.0), axis=-1)
    chosen_max = jnp.max(chosen, axis=-1, keepdims=True)
    chosen_exp = jnp.exp(chosen - chosen_max)
    gates_top = chosen_exp / jnp.sum(chosen_exp, axis=-1, keepdims=True)
    gate_weight = gates_top * keep_float
    cot_rows = cotangent[0].reshape(tokens, channels)
    flat_hot = one_hot.reshape(tokens * TOP, EXPERTS).astype(jnp.int32)
    running = jnp.cumsum(flat_hot, axis=0) - flat_hot
    slot_index = jnp.sum(running * flat_hot, axis=-1)
    flat_ids = route_ids.reshape(-1)
    destination = (
        flat_ids % local_experts * group_count + flat_ids // local_experts
    ) * CAP + slot_index
    slot_total = local_experts * group_count * CAP
    choice_norm = jnp.broadcast_to(normed[:, None, :], (tokens, TOP, channels)).reshape(
        tokens * TOP, channels
    )
    choice_cot = jnp.broadcast_to(cot_rows[:, None, :], (tokens, TOP, channels)).reshape(
        tokens * TOP, channels
    )
    send_norm = (
        jnp.zeros((slot_total, channels), jnp.bfloat16)
        .at[destination]
        .set(choice_norm)
        .reshape(local_experts, group_count, CAP, channels)
    )
    send_cot = (
        jnp.zeros((slot_total, channels), jnp.bfloat16)
        .at[destination]
        .set(choice_cot)
        .reshape(local_experts, group_count, CAP, channels)
    )
    send_gate = (
        jnp.zeros((slot_total,), jnp.float32)
        .at[destination]
        .set(gate_weight.reshape(tokens * TOP))
        .reshape(local_experts, group_count, CAP)
    )
    recv_norm, recv_cot, recv_gate = (
        lax.all_to_all(send_norm, "expert", split_axis=1, concat_axis=1, tiled=True),
        lax.all_to_all(send_cot, "expert", split_axis=1, concat_axis=1, tiled=True),
        lax.all_to_all(send_gate, "expert", split_axis=1, concat_axis=1, tiled=True),
    )
    expert_rows = group_count * CAP
    in_rows = recv_norm.reshape(local_experts, expert_rows, channels)
    cot_in = recv_cot.reshape(local_experts, expert_rows, channels)
    gate_in = recv_gate.reshape(local_experts, expert_rows)
    norm_piece = lax.all_gather(in_rows, "space", axis=1, tiled=True)
    cot_piece = lax.all_gather(cot_in, "space", axis=1, tiled=True)
    gate_piece = lax.all_gather(gate_in, "space", axis=1, tiled=True)[:, :, None]
    pre_own = jnp.einsum("erc,ecf->erf", norm_piece, up_weight, preferred_element_type=jnp.float32)
    act_own, slope_own = gelu_pair(pre_own)
    drive = jnp.einsum("erc,ecf->erf", cot_piece, down_weight, preferred_element_type=jnp.float32)
    act_bf = act_own.astype(jnp.bfloat16)
    dots_own = jnp.sum(act_bf.astype(jnp.float32) * drive, axis=-1)
    grad_own = (gate_piece * drive * slope_own).astype(jnp.bfloat16)
    act_gated = (gate_piece * act_own).astype(jnp.bfloat16)
    back_own = jnp.einsum(
        "erf,ecf->erc", grad_own, up_weight, preferred_element_type=jnp.float32
    ).astype(jnp.bfloat16)
    back_sum = lax.psum_scatter(back_own, "space", scatter_dimension=1, tiled=True)
    row_dots = lax.psum_scatter(dots_own, "space", scatter_dimension=1, tiled=True)
    up_total = jnp.einsum("erc,erf->ecf", norm_piece, grad_own, preferred_element_type=jnp.float32)
    down_total = jnp.einsum("erc,erf->ecf", cot_piece, act_gated, preferred_element_type=jnp.float32)
    back_grad = back_sum.reshape(local_experts, group_count, CAP, channels)
    ret_grad, ret_dots = (
        lax.all_to_all(back_grad, "expert", split_axis=1, concat_axis=1, tiled=True),
        lax.all_to_all(
            row_dots.reshape(local_experts, group_count, CAP),
            "expert",
            split_axis=1,
            concat_axis=1,
            tiled=True,
        ),
    )
    choice_grad = (
        ret_grad.reshape(slot_total, channels)[destination]
        .astype(jnp.float32)
        .reshape(tokens, TOP, channels)
    )
    norm_grad = jnp.sum(choice_grad, axis=1)
    inner_mean = jnp.mean(norm_grad * norm_float, axis=-1, keepdims=True)
    residual_grad = (
        cot_rows.astype(jnp.float32) + (norm_grad - norm_float * inner_mean) / rms_value
    ).astype(jnp.bfloat16)
    choice_dots = ret_dots.reshape(slot_total)[destination].astype(jnp.float32).reshape(tokens, TOP)
    gate_drive = keep_float * choice_dots
    gate_mix = jnp.sum(gates_top * gate_drive, axis=-1, keepdims=True)
    gate_part = gates_top * (gate_drive - gate_mix)
    logit_gate = jnp.sum(jnp.where(one_hot, gate_part[:, :, None], 0.0), axis=1)
    expert_share = jnp.sum(jnp.where(one_hot, keep_float[:, :, None], 0.0), axis=(0, 1)) / (
        TOP * tokens
    )
    logit_max = jnp.max(router_logits, axis=-1, keepdims=True)
    logit_exp = jnp.exp(router_logits - logit_max)
    router_probs = logit_exp / jnp.sum(logit_exp, axis=-1, keepdims=True)
    share_mean = jnp.sum(router_probs * expert_share[None, :], axis=-1, keepdims=True)
    balance = EXPERTS * router_probs * (expert_share[None, :] - share_mean)
    logit_grad = (logit_gate + balance).reshape(1, win_side, map_width, EXPERTS)
    grad_map = residual_grad.reshape(win_side, map_width, channels)
    next_grad = from_behind(grad_map[:half_win], "space", -1)
    grad_shifted = jnp.concatenate([grad_map[half_win:], next_grad], axis=0)
    last_flags = jnp.reshape(space_index == space_count - 1, (1,))
    frame_grads = window_grads(qkv_shifted[:, None], grad_shifted[None], last_flags, HEADS)[:, 0]
    prev_rows = from_behind(frame_grads[:, half_win:], "space", 1)
    attn_grad = jnp.concatenate([prev_rows, frame_grads[:, :half_win]], axis=1)
    return (attn_grad[:, None], grad_map[None], up_total, down_total, logit_grad)


META = 8
PAD = 16
GELU_C = math.sqrt(2.0 / math.pi)
GELU_A = 0.044715


def iota(shape, dim):
    return lax.broadcasted_iota(jnp.int32, shape, dim)


def dot(a, b, ca, cb):
    return lax.dot_general(a, b, (((ca,), (cb,)), ((), ())), preferred_element_type=jnp.float32)


def to_lanes(column):
    n = column.shape[0]
    return jnp.sum(jnp.where(iota((n, n), 0) == iota((n, n), 1), column, 0.0), axis=0, keepdims=True)


def to_rows(row):
    n = row.shape[1]
    return jnp.sum(jnp.where(iota((n, n), 0) == iota((n, n), 1), row, 0.0), axis=1, keepdims=True)


def stack_rows(rows):
    out = jnp.zeros((META, rows[0].shape[1]), jnp.float32)
    sub = iota(out.shape, 0)
    for k, row in enumerate(rows):
        out = jnp.where(sub == k, row, out)
    return out


def split_hi_lo(x):
    hi = x.astype(jnp.bfloat16).astype(jnp.float32)
    return hi, x - hi


def routing(logits, ids):
    cols = iota(logits.shape, 1).astype(jnp.float32)
    hot = [cols == ids[k] for k in range(TOP)]
    z = [jnp.sum(jnp.where(h, logits, 0.0), axis=-1, keepdims=True) for h in hot]
    top = jnp.maximum(z[0], z[1])
    ex = [jnp.exp(v - top) for v in z]
    total = ex[0] + ex[1]
    return hot, [v / total for v in ex]


def flatten(ref, rows_ref, first=0, count=None):
    side = ref.shape[1]
    for i in range(count or ref.shape[0]):
        rows_ref[i * side : (i + 1) * side, :] = ref[first + i].astype(jnp.float32)


def column(ref, k):
    rows, _, side = ref.shape
    line = iota((rows * side, rows), 0)
    spread = jnp.where(line // side == iota((rows * side, rows), 1), 1.0, 0.0).astype(jnp.bfloat16)
    wide = dot(spread, ref[:, k, :].astype(jnp.float32).astype(jnp.bfloat16), 1, 0)
    own = iota(wide.shape, 0) % side == iota(wide.shape, 1)
    return jnp.sum(jnp.where(own, wide, 0.0), axis=1, keepdims=True)


def halve_kernel(x_ref, up_ref, low_ref, rows_ref):
    side = x_ref.shape[1] // 2
    for n in range(x_ref.shape[0]):
        for at, out in ((0, up_ref), (side, low_ref)):
            flatten(x_ref.at[n], rows_ref, at, side)
            out[n] = rows_ref[...].astype(jnp.bfloat16)


def prep_kernel(res_ref, log_ref, ids_ref, keep_ref, cot_ref, out_ref, flat_ref, cols_ref, rows_ref):
    tokens, channels = rows_ref.shape
    flatten(cot_ref, rows_ref)
    out_ref[1, :tokens, :] = rows_ref[...].astype(jnp.bfloat16)
    flatten(res_ref, rows_ref)
    res = rows_ref[...]
    flat_ref[...] = res.astype(jnp.bfloat16)
    rms = jnp.sqrt(jnp.mean(res * res, axis=-1, keepdims=True) + NORM_EPS)
    out_ref[0, :tokens, :] = (res / rms).astype(jnp.bfloat16)
    cols = [column(ref, k) for ref in (ids_ref, keep_ref) for k in range(TOP)]
    lane = iota(cols_ref.shape, 1)
    table = jnp.zeros(cols_ref.shape, jnp.float32)
    for n, c in enumerate(cols):
        table = jnp.where(lane == n, c, table)
    cols_ref[...] = table
    ids, keep = cols[:TOP], cols[TOP:]
    hot, gates = routing(log_ref[...], ids)
    both = jnp.where(hot[0] | hot[1], 1.0, 0.0).astype(jnp.bfloat16)
    earlier = jnp.where(iota((tokens, tokens), 1) < iota((tokens, tokens), 0), 1.0, 0.0)
    count = dot(earlier.astype(jnp.bfloat16), both, 1, 0)
    where, weight = [], []
    for k in range(TOP):
        slot = jnp.sum(jnp.where(hot[k], count, 0.0), axis=-1, keepdims=True)
        where += [ids[k], slot]
        weight += split_hi_lo(gates[k] * keep[k])
    for side, cols in ((0, where), (1, weight)):
        out_ref[side, tokens:, :] = jnp.zeros((META, channels), jnp.bfloat16)
        rows = stack_rows([to_lanes(c) for c in cols])
        out_ref[side, tokens:, :tokens] = rows.astype(jnp.bfloat16)


def ffn_kernel(table, tokens, base_ref, *refs):
    used = 1 + max(max(t[0], t[2]) for t in table)
    tok_refs = refs[:used]
    up_ref, down_ref = refs[used : used + 2]
    mine_ref, part_ref, x_ref, pg_ref, ag_ref = refs[used + 2 : used + 7]
    xs, gs, ds, rs = refs[used + 7 :]
    rows = xs.shape[1]
    channels = up_ref.shape[1]
    half = channels // 2
    step = pl.program_id(0)
    strips = [(tok_refs[a], i, tok_refs[b], j, who, to) for a, i, b, j, who, to in table]

    def choices(ref, n_at):
        meta = ref[n_at, tokens:, :].astype(jnp.float32)[:, :tokens]
        base = base_ref[0].astype(jnp.float32)
        line = iota((rows, tokens), 0).astype(jnp.float32)
        return [
            line == (meta[2 * k : 2 * k + 1] - base) * PAD + meta[2 * k + 1 : 2 * k + 2]
            for k in range(TOP)
        ]

    @pl.when(step == 0)
    def _():
        for i, (ref, n_at, cref, c_at, _, _) in enumerate(strips):
            picks = choices(ref, n_at)
            pick = jnp.where(picks[0] | picks[1], 1.0, 0.0).astype(jnp.bfloat16)
            gate = cref[c_at, tokens:, :].astype(jnp.float32)[:, :tokens]
            xs[i, :, :channels] = dot(pick, ref[n_at, :tokens, :], 1, 0).astype(jnp.bfloat16)
            xs[i, :, channels:] = dot(pick, cref[c_at, :tokens, :], 1, 0).astype(jnp.bfloat16)
            weight = sum(
                jnp.where(picks[k], gate[2 * k : 2 * k + 1] + gate[2 * k + 1 : 2 * k + 2], 0.0)
                for k in range(TOP)
            )
            gs[i] = jnp.sum(weight, axis=1, keepdims=True)

    count = len(strips) * PAD
    at = pl.ds(pl.multiple_of(step * PAD, PAD), PAD)
    x = xs[:, at, :].reshape(count, 2 * channels)
    g = gs[:, at, :].reshape(count, 1)
    x_ref[0] = x
    pre = dot(x[:, :channels], up_ref[0], 1, 0)
    drive = dot(x[:, channels:], down_ref[0], 1, 0)
    sq = pre * pre
    t = jnp.tanh(GELU_C * (pre + GELU_A * (sq * pre)))
    act = 0.5 * pre * (1.0 + t)
    slope = 0.5 * (1.0 + t) + 0.5 * pre * (1.0 - t * t) * (GELU_C * (1.0 + 3.0 * GELU_A * sq))
    dots = jnp.sum(act.astype(jnp.bfloat16).astype(jnp.float32) * drive, axis=1, keepdims=True)
    ds[:, at, :] = dots.reshape(len(strips), PAD, 1)
    ag_ref[0] = (g * act).astype(jnp.bfloat16)
    pg = (g * drive * slope).astype(jnp.bfloat16)
    pg_ref[0] = pg
    back = dot(pg, up_ref[0], 1, 1).astype(jnp.bfloat16)
    rs[:, at, :] = back.reshape(len(strips), PAD, channels)

    @pl.when(step == pl.num_programs(0) - 1)
    def _():
        for i, (ref, n_at, _, _, who, to) in enumerate(strips):
            picks = choices(ref, n_at)
            pick = jnp.where(picks[0] | picks[1], 1.0, 0.0).astype(jnp.bfloat16)
            grad = dot(pick, rs[i], 0, 0).astype(jnp.bfloat16)
            d = [jnp.sum(jnp.where(p, ds[i], 0.0), axis=0, keepdims=True) for p in picks]
            d = [split_hi_lo(v) for v in d]
            out = mine_ref if who == 0 else part_ref
            for h in range(2):
                out[h, to, :tokens, :] = grad[:, h * half : (h + 1) * half]
                out[h, to, tokens:, :] = jnp.zeros((META, half), jnp.bfloat16)
            rows_d = stack_rows([d[0][0], d[1][0], d[0][1], d[1][1]])
            out[0, to, tokens:, :tokens] = rows_d.astype(jnp.bfloat16)


def run_ffn(base, toks, table, up, down, tokens):
    experts, channels, hidden = up.shape
    strips = len(table)
    count = strips * PAD
    half = channels // 2
    whole = lambda shape: pl.BlockSpec(shape, lambda j: (0,) * len(shape))
    each = lambda shape: pl.BlockSpec((1,) + shape, lambda j: (j,) + (0,) * len(shape))
    out_t = (2, strips // 2, tokens + META, half)
    bf = jnp.bfloat16
    return pl.pallas_call(
        functools.partial(ffn_kernel, table, tokens),
        grid=(experts,),
        out_shape=[
            jax.ShapeDtypeStruct(out_t, bf),
            jax.ShapeDtypeStruct(out_t, bf),
            jax.ShapeDtypeStruct((experts, count, 2 * channels), bf),
            jax.ShapeDtypeStruct((experts, count, hidden), bf),
            jax.ShapeDtypeStruct((experts, count, hidden), bf),
        ],
        in_specs=[pl.BlockSpec(memory_space=pltpu.SMEM)]
        + [whole(a.shape) for a in toks]
        + [each((channels, hidden))] * 2,
        out_specs=[
            whole(out_t),
            whole(out_t),
            each((count, 2 * channels)),
            each((count, hidden)),
            each((count, hidden)),
        ],
        scratch_shapes=[
            pltpu.VMEM((strips, experts * PAD, 2 * channels), bf),
            pltpu.VMEM((strips, experts * PAD, 1), jnp.float32),
            pltpu.VMEM((strips, experts * PAD, 1), jnp.float32),
            pltpu.VMEM((strips, experts * PAD, channels), bf),
        ],
        compiler_params=pltpu.CompilerParams(dimension_semantics=("arbitrary",)),
        cost_estimate=pl.CostEstimate(
            flops=12 * experts * count * channels * hidden,
            bytes_accessed=8 * up.size + count * 4096 * experts,
            transcendentals=0,
        ),
        name="ffn",
    )(base, *toks, up, down)


def wgrad_kernel(n, keep, *refs):
    refs = refs[keep:]
    xs, pgs, ags = refs[:n], refs[n : 2 * n], refs[2 * n : 3 * n]
    up_ref, down_ref = refs[3 * n :]
    channels = up_ref.shape[1]
    up = down = 0.0
    for x, pg, ag in zip(xs, pgs, ags):
        up = up + dot(x[0, :, :channels], pg[0], 0, 0)
        down = down + dot(x[0, :, channels:], ag[0], 0, 0)
    up_ref[0] = up
    down_ref[0] = down


def run_wgrad(xs, pgs, ags, first, last, before=()):
    experts, _, two = xs[0].shape
    hidden = pgs[0].shape[2]
    each = lambda shape: pl.BlockSpec((1,) + shape[1:], lambda j: (j + first, 0, 0))
    out = (experts, two // 2, hidden)
    ops = list(xs) + list(pgs) + list(ags)
    rows = sum(x.shape[1] for x in xs)
    return pl.pallas_call(
        functools.partial(wgrad_kernel, len(xs), len(before)),
        grid=(last - first,),
        out_shape=[jax.ShapeDtypeStruct(out, jnp.float32)] * 2,
        in_specs=[pl.BlockSpec(memory_space=pl.ANY)] * len(before) + [each(a.shape) for a in ops],
        out_specs=[each(out)] * 2,
        input_output_aliases={i: i for i in range(len(before))},
        compiler_params=pltpu.CompilerParams(dimension_semantics=("arbitrary",)),
        cost_estimate=pl.CostEstimate(
            flops=2 * (last - first) * rows * two * hidden,
            bytes_accessed=(last - first) * (sum(a.size * 2 for a in ops) // experts + 4 * two * hidden),
            transcendentals=0,
        ),
        name="wgrad",
    )(*before, *ops)


def add_blocks(a, b, tokens):
    s = a.astype(jnp.float32) + b.astype(jnp.float32)
    return s[:tokens].astype(jnp.bfloat16), meta_sum(s[tokens:]).astype(jnp.bfloat16)


def meta_sum(s):
    total = s + pltpu.roll(s, META - TOP, 0)
    hi, lo = split_hi_lo(total)
    sub = iota(s.shape, 0)
    return jnp.where(sub < TOP, hi, jnp.where(sub < 2 * TOP, pltpu.roll(lo, TOP, 0), 0.0))


def put(ref, at, a, b, tokens):
    body, meta = add_blocks(a, b, tokens)
    ref[at, :tokens, :] = body
    ref[at, tokens:, :] = meta


def core_sum_kernel(chunks, tokens, *refs):
    k1_ref, s1_ref, k2_ref, s2_ref = refs[2 * chunks :]
    for c in range(chunks):
        mine_ref, got_ref = refs[2 * c : 2 * c + 2]
        for y in range(2):
            for x in range(2):
                i = y * 2 + x
                put((k1_ref, s1_ref)[x], c * 2 + y, mine_ref[0, i], got_ref[0, i], tokens)
                put((k2_ref, s2_ref)[y], c * 2 + x, mine_ref[1, i], got_ref[1, i], tokens)


def pair_sum_kernel(chunks, tokens, a1, b1, a2, b2, k1_ref, s1_ref, k2_ref, s2_ref):
    for c in range(chunks):
        for u in range(2):
            i = c * 2 + u
            put((k1_ref, s1_ref)[u], c, a1[i], b1[i], tokens)
            put((k2_ref, s2_ref)[u], c, a2[i], b2[i], tokens)


def last_sum_kernel(tokens, a1, b1, a2, b2, *outs):
    for c, ref in enumerate(outs):
        put(ref, 0, a1[c], b1[c], tokens)
        put(ref, 1, a2[c], b2[c], tokens)


def vmem_call(kernel, outs, *ops, scratch=()):
    full = pl.BlockSpec(memory_space=pltpu.VMEM)
    size = sum(a.size * a.dtype.itemsize for a in list(ops) + list(outs))
    return pl.pallas_call(
        kernel,
        out_shape=outs,
        in_specs=[full] * len(ops),
        out_specs=[full] * len(outs),
        scratch_shapes=list(scratch),
        cost_estimate=pl.CostEstimate(flops=size, bytes_accessed=size, transcendentals=0),
    )(*ops)


def final_kernel(n, res_ref, blk_ref, log_ref, cols_ref, *refs):
    parts = refs[:n]
    up_ref, low_ref, map_ref, log_out, rows_ref = refs[n:]
    tokens, _ = res_ref.shape
    res = res_ref[...].astype(jnp.float32)
    rms = jnp.sqrt(jnp.mean(res * res, axis=-1, keepdims=True) + NORM_EPS)
    nf = res / rms
    halves = [sum(p[h].astype(jnp.float32) for p in parts) for h in range(2)]
    grad = jnp.concatenate([h[:tokens] for h in halves], axis=1)
    inner = jnp.mean(grad * nf, axis=-1, keepdims=True)
    cot = blk_ref[1, :tokens, :].astype(jnp.float32)
    out = cot + (grad - nf * inner) / rms
    mid = tokens // 2
    up_ref[...] = out[:mid].astype(jnp.bfloat16)
    low_ref[...] = out[mid:].astype(jnp.bfloat16)
    rows_ref[...] = out
    side = map_ref.shape[1]
    for i in range(map_ref.shape[0]):
        map_ref[i] = rows_ref[i * side : (i + 1) * side, :].astype(jnp.bfloat16)
    meta = halves[0][tokens:]
    total = (meta + pltpu.roll(meta, META - TOP, 0))[:, :tokens]
    logits = log_ref[...]
    experts = logits.shape[1]
    cols = [cols_ref[:, k : k + 1] for k in range(2 * TOP)]
    keeps = cols[TOP:]
    hot, gates = routing(logits, cols[:TOP])
    dots = [to_rows(total[k : k + 1]).astype(jnp.bfloat16).astype(jnp.float32) for k in range(TOP)]
    drive = [keeps[k] * dots[k] for k in range(TOP)]
    mix = gates[0] * drive[0] + gates[1] * drive[1]
    part = sum(jnp.where(hot[k], gates[k] * (drive[k] - mix), 0.0) for k in range(TOP))
    share = sum(
        jnp.sum(jnp.where(hot[k], keeps[k], 0.0), axis=0, keepdims=True) for k in range(TOP)
    ) / (TOP * tokens)
    top = jnp.max(logits, axis=-1, keepdims=True)
    ex = jnp.exp(logits - top)
    probs = ex / jnp.sum(ex, axis=-1, keepdims=True)
    mean = jnp.sum(probs * share, axis=-1, keepdims=True)
    log_out[...] = part + experts * probs * (share - mean)


def attn_kernel(heads, side, at_ref, up, low, after, before, gu, gl, gafter, gbefore, out_ref):
    mid, width = gu.shape
    area = 2 * mid
    dim = width // heads
    inv = dim**-0.5
    first = pl.program_id(0) == 0
    wide = lambda r: r.astype(jnp.float32)
    window = lambda l, a, b, u: jnp.concatenate(
        [jnp.where(first, wide(l), wide(b)), jnp.where(first, wide(a), wide(u))], axis=0
    ).astype(jnp.bfloat16)
    q, k, v = [window(low[n], after[n], before[n], up[n]) for n in range(3)]
    g = window(gl[...], gafter[...], gbefore[...], gu[...])
    lane = iota((area, width), 1) // dim
    masks = [jnp.where(lane == h, 1.0, 0.0) for h in range(heads)]
    spread = lambda a: jnp.concatenate([a * m.astype(jnp.bfloat16) for m in masks], axis=0)
    qs, gsp = spread(q), spread(g)
    last = jnp.where(first, at_ref[0], at_ref[1]).astype(jnp.float32)

    def label(at):
        at = at % area
        col = jnp.where(at % side >= side // 2, 1.0, 0.0)
        return col + jnp.where(at >= mid, 2.0 * last, 0.0)

    away = label(iota((area, 1), 0)) != label(iota((1, heads * area), 1))
    scores = dot(k, qs, 1, 1) * inv + jnp.where(away, SCORE_MASK, 0.0)
    ex = jnp.exp(scores - jnp.max(scores, axis=0, keepdims=True))
    probs = ex * (1.0 / jnp.sum(ex, axis=0, keepdims=True))
    weights = probs.astype(jnp.bfloat16)
    pgrad = dot(v, gsp, 1, 1)
    delta = jnp.sum(weights.astype(jnp.float32) * pgrad, axis=0, keepdims=True)
    sgrad = (probs * (pgrad - delta)).astype(jnp.bfloat16)
    dk = dot(sgrad, qs, 1, 0) * inv
    dv = dot(weights, gsp, 1, 0)
    broad = dot(sgrad, k, 0, 0)
    dq = sum(broad[h * area : (h + 1) * area] * masks[h] for h in range(heads)) * inv
    for n, a in enumerate((dq, dk, dv)):
        own = jnp.where(first, a[:mid], a[mid:])
        for i in range(mid // side):
            out_ref[n, i] = own[i * side : (i + 1) * side].astype(jnp.bfloat16)


def run_attention(at, halves, grads, side, groups):
    _, mid, channels = halves[0].shape
    width = channels // groups
    heads = HEADS // groups
    rows = mid // side
    return pl.pallas_call(
        functools.partial(attn_kernel, heads, side),
        grid=(2, groups),
        out_shape=jax.ShapeDtypeStruct((3, 2 * rows, side, channels), jnp.bfloat16),
        in_specs=[pl.BlockSpec(memory_space=pltpu.SMEM)]
        + [pl.BlockSpec((3, mid, width), lambda w, g: (0, 0, g))] * 4
        + [pl.BlockSpec((mid, width), lambda w, g: (0, g))] * 4,
        out_specs=pl.BlockSpec((3, rows, side, width), lambda w, g: (0, 1 - w, 0, g)),
        compiler_params=pltpu.CompilerParams(dimension_semantics=("arbitrary", "arbitrary")),
        cost_estimate=pl.CostEstimate(
            flops=40 * mid * mid * channels * heads, bytes_accessed=64 * mid * channels, transcendentals=0
        ),
        name="attn",
    )(at, *halves, *grads)


def per_device_tokens(
    attn_inputs, residual, logits, expert_ids, keep_mask, cotangent, up_weight, down_weight
):
    n_exp, n_space = lax.axis_size("expert"), lax.axis_size("space")
    local = up_weight.shape[0]
    win_side, map_width, channels = residual.shape[1:]
    tokens = win_side * map_width
    mid = tokens // 2
    deep = n_space // 2

    def send(block, dz=0, dx=0, dy=0, dc=0):
        pairs = []
        for e in range(n_exp):
            for s in range(n_space):
                y, c, z, x = e // 2, e % 2, s // 2, s % 2
                to_e = (y + dy) % (n_exp // 2) * 2 + (c + dc) % 2
                to_s = (z + dz) % deep * 2 + (x + dx) % 2
                pairs.append((e * n_space + s, to_e * n_space + to_s))
        return lax.ppermute(block, ("expert", "space"), pairs)

    def neighbour(block, distance):
        return from_behind(block, "space", distance)

    bf = jnp.bfloat16
    deal = jax.ShapeDtypeStruct
    rows = tokens + META
    half = channels // 2
    third = deal((3, mid, channels), bf)
    q_up, q_low = vmem_call(
        halve_kernel, [third, third], attn_inputs[:, 0],
        scratch=[pltpu.VMEM((mid, channels), jnp.float32)],
    )
    q_after = neighbour(q_up, -1)
    q_before = neighbour(q_low, 1)
    log = logits[0].reshape(tokens, EXPERTS)
    turned = lambda a: a[0].transpose(0, 2, 1)
    flat_rows = pltpu.VMEM((tokens, channels), jnp.float32)
    block, flat, cols = vmem_call(
        prep_kernel,
        [deal((2, rows, channels), bf), deal((tokens, channels), bf), deal((tokens, META), jnp.float32)],
        residual[0], log, turned(expert_ids), turned(keep_mask), cotangent[0],
        scratch=[flat_rows],
    )

    base = jnp.reshape(lax.axis_index("expert") * local, (1,)).astype(jnp.int32)
    moved = [block] + [send(block, dz=d) for d in range(1, deep)]
    xs, pgs, ags, sums = [], [], [], []
    for d in range(deep):
        own = moved[d]
        x = send(own, dx=1)
        y = send(own, dy=1)
        if d == deep - 1:
            diag = [send(x[:1], dy=1), send(y[1:], dx=1)]
        else:
            diag = [send(x, dy=1) if d % 2 == 0 else send(y, dx=1)]
        toks, table = [], []
        for who in range(2):
            got = [own, x, y] + diag
            if who:
                got = [send(a, dc=1) for a in got]
            at = len(toks)
            toks += got
            table += [(at + i, 0, at + i, 1, who, i) for i in range(3)]
            table.append((at + 3, 0, at + 2 + len(diag), 1 if len(diag) == 1 else 0, who, 3))
        t_mine, t_part, xd, pg, ag = run_ffn(base, toks, table, up_weight, down_weight, tokens)
        xs.append(xd)
        pgs.append(pg)
        ags.append(ag)
        sums.append((t_mine, send(t_part, dc=1)))

    parts = []
    for group in (range(deep - 1), range(deep - 1, deep)):
        n = len(group)
        two = deal((2 * n, rows, half), bf)
        k1, s1, k2, s2 = vmem_call(
            functools.partial(core_sum_kernel, n, tokens),
            [two] * 4,
            *[a for d in group for a in sums[d]],
        )
        r1, r2 = send(s1, dx=1), send(s2, dy=1)
        one = deal((n, rows, half), bf)
        k1, s1, k2, s2 = vmem_call(
            functools.partial(pair_sum_kernel, n, tokens), [one] * 4, k1, r1, k2, r2
        )
        r1, r2 = send(s1, dy=1), send(s2, dx=1)
        done = vmem_call(
            functools.partial(last_sum_kernel, tokens),
            [deal((2, rows, half), bf)] * n,
            k1, r1, k2, r2,
        )
        for d, w in zip(group, done):
            parts.append(w if d == 0 else send(w, dz=-d))
    cuts = [local * i // WGRAD_PIECES for i in range(WGRAD_PIECES + 1)]
    totals = ()
    for i in range(WGRAD_PIECES):
        totals = run_wgrad(xs, pgs, ags, cuts[i], cuts[i + 1], totals)

    g_up, g_low, g_map, logit_grad = vmem_call(
        functools.partial(final_kernel, deep),
        [deal((mid, channels), bf)] * 2
        + [deal((win_side, map_width, channels), bf), deal((tokens, EXPERTS), jnp.float32)],
        flat, block, log, cols, *parts,
        scratch=[flat_rows],
    )
    g_after = neighbour(g_up, -1)
    g_before = neighbour(g_low, 1)
    space = lax.axis_index("space")
    last = jnp.stack([space == n_space - 1, space == 0]).astype(jnp.int32)
    grads = run_attention(
        last, (q_up, q_low, q_after, q_before), (g_up, g_low, g_after, g_before), map_width, 2
    )
    return (
        grads[:, None],
        g_map[None],
        *totals,
        logit_grad.reshape(1, win_side, map_width, EXPERTS),
    )


WGRAD_PIECES = 3


def solution(mesh):
    n_exp, n_space = mesh.shape["expert"], mesh.shape["space"]
    local = EXPERTS // n_exp
    gather_tokens = n_exp // 2 == 2 and n_space % 2 == 0 and n_space // 2 > 2 and 2 * local * CAP >= TOKENS

    def per_device(*args):
        return per_device_tokens(*args)

    in_specs = (
        P(None, "expert", "space", None, None),
        P("expert", "space", None, None),
        P("expert", "space", None, None),
        P("expert", "space", None, None),
        P("expert", "space", None, None),
        P("expert", "space", None, None),
        P("expert", None, "space"),
        P("expert", None, "space"),
    )
    out_specs = (
        P(None, "expert", "space", None, None),
        P("expert", "space", None, None),
        P("expert", None, "space"),
        P("expert", None, "space"),
        P("expert", "space", None, None),
    )
    return jax.shard_map(
        per_device if gather_tokens else per_device_slots,
        mesh=mesh, in_specs=in_specs, out_specs=out_specs, check_vma=False,
    )
```

```python
import functools
import math

import jax
import jax.numpy as jnp
from jax import lax
from jax.experimental import pallas as pl
from jax.experimental.pallas import tpu as pltpu
from jax.sharding import PartitionSpec as P


HEADS = 16
EXPERTS = 32
TOP = 2
CAP = 12
TOKENS = 144


NORM_EPS = 1e-06
SCORE_MASK = -100.0


def from_behind(block, axis, distance):
    devices = range(lax.axis_size(axis))
    route = [((i - distance) % len(devices), i) for i in devices]
    return lax.ppermute(block, axis, route)


def gelu_pair(pre_act):
    activation, pullback = jax.vjp(jax.nn.gelu, pre_act)
    gelu_slope = pullback(jnp.ones_like(pre_act))[0]
    return (activation, gelu_slope)


def to_windows(tensor, head_count):
    blocks, win_side, map_width, channels = tensor.shape
    win_count = map_width // win_side
    head_dim = channels // head_count
    shaped = tensor.reshape(blocks, win_side, win_count, win_side, head_count, head_dim)
    shaped = shaped.transpose(0, 2, 4, 1, 3, 5)
    return shaped.reshape(blocks, win_count, head_count, win_side * win_side, head_dim)


def from_windows(tensor, win_side):
    blocks, win_count, head_count, _, head_dim = tensor.shape
    shaped = tensor.reshape(blocks, win_count, head_count, win_side, win_side, head_dim)
    shaped = shaped.transpose(0, 3, 1, 4, 2, 5)
    return shaped.reshape(blocks, win_side, win_count * win_side, head_count * head_dim)


def window_grads(frame_qkv, frame_grad, last_flags, head_count):
    win_side = frame_grad.shape[1]
    map_width = frame_grad.shape[2]
    half_win = win_side // 2
    head_dim = frame_grad.shape[3] // head_count
    inv_sqrt = head_dim ** (-0.5)
    rolled = jnp.roll(frame_qkv, -half_win, axis=3)
    grad_rolled = jnp.roll(frame_grad, -half_win, axis=2)
    query_win = to_windows(rolled[0], head_count)
    key_win = to_windows(rolled[1], head_count)
    value_win = to_windows(rolled[2], head_count)
    grad_win = to_windows(grad_rolled, head_count)
    row_pos = jnp.arange(win_side, dtype=jnp.int32)
    col_pos = jnp.arange(map_width, dtype=jnp.int32)
    row_label = jnp.where(last_flags[:, None], jnp.where(row_pos < half_win, 1, 2)[None, :], 0)
    col_label = jnp.where(
        col_pos >= map_width - win_side, jnp.where(col_pos < map_width - half_win, 1, 2), 0
    )
    region = 3 * row_label[:, :, None] + col_label[None, None, :]
    region = region.reshape(region.shape[0], win_side, map_width // win_side, win_side).transpose(
        0, 2, 1, 3
    )
    region = region.reshape(region.shape[0], region.shape[1], win_side * win_side)
    score_bias = jnp.where(region[:, :, :, None] != region[:, :, None, :], SCORE_MASK, 0.0)[
        :, :, None
    ]
    scores = (
        jnp.einsum("bnhqd,bnhkd->bnhqk", query_win, key_win, preferred_element_type=jnp.float32)
        * inv_sqrt
        + score_bias
    )
    row_max = jnp.max(scores, axis=-1, keepdims=True)
    exp_scores = jnp.exp(scores - row_max)
    attn_probs = exp_scores / jnp.sum(exp_scores, axis=-1, keepdims=True)
    weights_bf = attn_probs.astype(jnp.bfloat16)
    attn_out = jnp.einsum(
        "bnhqk,bnhkd->bnhqd", weights_bf, value_win, preferred_element_type=jnp.float32
    )
    row_delta = jnp.sum(grad_win.astype(jnp.float32) * attn_out, axis=-1, keepdims=True)
    prob_grad = jnp.einsum(
        "bnhqd,bnhkd->bnhqk", grad_win, value_win, preferred_element_type=jnp.float32
    )
    score_grad = (attn_probs * (prob_grad - row_delta)).astype(jnp.bfloat16)
    query_grad = (
        jnp.einsum("bnhqk,bnhkd->bnhqd", score_grad, key_win, preferred_element_type=jnp.float32)
        * inv_sqrt
    ).astype(jnp.bfloat16)
    key_grad = (
        jnp.einsum("bnhqk,bnhqd->bnhkd", score_grad, query_win, preferred_element_type=jnp.float32)
        * inv_sqrt
    ).astype(jnp.bfloat16)
    value_grad = jnp.einsum(
        "bnhqk,bnhqd->bnhkd", weights_bf, grad_win, preferred_element_type=jnp.float32
    ).astype(jnp.bfloat16)
    stacked = jnp.stack(
        [
            from_windows(query_grad, win_side),
            from_windows(key_grad, win_side),
            from_windows(value_grad, win_side),
        ]
    )
    return jnp.roll(stacked, half_win, axis=3)


def per_device_slots(
    attn_inputs, residual, logits, expert_ids, keep_mask, cotangent, up_weight, down_weight
):
    group_count = lax.axis_size("expert")
    local_experts = up_weight.shape[0]
    win_side = residual.shape[1]
    map_width = residual.shape[2]
    channels = residual.shape[3]
    tokens = win_side * map_width
    half_win = win_side // 2
    space_index = lax.axis_index("space")
    space_count = lax.axis_size("space")
    qkv_local = attn_inputs[:, 0]
    next_rows = from_behind(qkv_local[:, :half_win], "space", -1)
    qkv_shifted = jnp.concatenate([qkv_local[:, half_win:], next_rows], axis=1)
    resid_float = residual[0].reshape(tokens, channels).astype(jnp.float32)
    rms_value = jnp.sqrt(jnp.mean(resid_float * resid_float, axis=-1, keepdims=True) + NORM_EPS)
    norm_float = resid_float / rms_value
    normed = norm_float.astype(jnp.bfloat16)
    route_ids = expert_ids[0].reshape(tokens, TOP)
    keep_float = keep_mask[0].reshape(tokens, TOP).astype(jnp.float32)
    router_logits = logits[0].reshape(tokens, EXPERTS)
    expert_cols = jnp.arange(EXPERTS, dtype=jnp.int32)
    one_hot = route_ids[:, :, None] == expert_cols[None, None, :]
    chosen = jnp.sum(jnp.where(one_hot, router_logits[:, None, :], 0.0), axis=-1)
    chosen_max = jnp.max(chosen, axis=-1, keepdims=True)
    chosen_exp = jnp.exp(chosen - chosen_max)
    gates_top = chosen_exp / jnp.sum(chosen_exp, axis=-1, keepdims=True)
    gate_weight = gates_top * keep_float
    cot_rows = cotangent[0].reshape(tokens, channels)
    flat_hot = one_hot.reshape(tokens * TOP, EXPERTS).astype(jnp.int32)
    running = jnp.cumsum(flat_hot, axis=0) - flat_hot
    slot_index = jnp.sum(running * flat_hot, axis=-1)
    flat_ids = route_ids.reshape(-1)
    destination = (
        flat_ids % local_experts * group_count + flat_ids // local_experts
    ) * CAP + slot_index
    slot_total = local_experts * group_count * CAP
    choice_norm = jnp.broadcast_to(normed[:, None, :], (tokens, TOP, channels)).reshape(
        tokens * TOP, channels
    )
    choice_cot = jnp.broadcast_to(cot_rows[:, None, :], (tokens, TOP, channels)).reshape(
        tokens * TOP, channels
    )
    send_norm = (
        jnp.zeros((slot_total, channels), jnp.bfloat16)
        .at[destination]
        .set(choice_norm)
        .reshape(local_experts, group_count, CAP, channels)
    )
    send_cot = (
        jnp.zeros((slot_total, channels), jnp.bfloat16)
        .at[destination]
        .set(choice_cot)
        .reshape(local_experts, group_count, CAP, channels)
    )
    send_gate = (
        jnp.zeros((slot_total,), jnp.float32)
        .at[destination]
        .set(gate_weight.reshape(tokens * TOP))
        .reshape(local_experts, group_count, CAP)
    )
    recv_norm, recv_cot, recv_gate = (
        lax.all_to_all(send_norm, "expert", split_axis=1, concat_axis=1, tiled=True),
        lax.all_to_all(send_cot, "expert", split_axis=1, concat_axis=1, tiled=True),
        lax.all_to_all(send_gate, "expert", split_axis=1, concat_axis=1, tiled=True),
    )
    expert_rows = group_count * CAP
    in_rows = recv_norm.reshape(local_experts, expert_rows, channels)
    cot_in = recv_cot.reshape(local_experts, expert_rows, channels)
    gate_in = recv_gate.reshape(local_experts, expert_rows)
    norm_piece = lax.all_gather(in_rows, "space", axis=1, tiled=True)
    cot_piece = lax.all_gather(cot_in, "space", axis=1, tiled=True)
    gate_piece = lax.all_gather(gate_in, "space", axis=1, tiled=True)[:, :, None]
    pre_own = jnp.einsum("erc,ecf->erf", norm_piece, up_weight, preferred_element_type=jnp.float32)
    act_own, slope_own = gelu_pair(pre_own)
    drive = jnp.einsum("erc,ecf->erf", cot_piece, down_weight, preferred_element_type=jnp.float32)
    act_bf = act_own.astype(jnp.bfloat16)
    dots_own = jnp.sum(act_bf.astype(jnp.float32) * drive, axis=-1)
    grad_own = (gate_piece * drive * slope_own).astype(jnp.bfloat16)
    act_gated = (gate_piece * act_own).astype(jnp.bfloat16)
    back_own = jnp.einsum(
        "erf,ecf->erc", grad_own, up_weight, preferred_element_type=jnp.float32
    ).astype(jnp.bfloat16)
    back_sum = lax.psum_scatter(back_own, "space", scatter_dimension=1, tiled=True)
    row_dots = lax.psum_scatter(dots_own, "space", scatter_dimension=1, tiled=True)
    up_total = jnp.einsum("erc,erf->ecf", norm_piece, grad_own, preferred_element_type=jnp.float32)
    down_total = jnp.einsum("erc,erf->ecf", cot_piece, act_gated, preferred_element_type=jnp.float32)
    back_grad = back_sum.reshape(local_experts, group_count, CAP, channels)
    ret_grad, ret_dots = (
        lax.all_to_all(back_grad, "expert", split_axis=1, concat_axis=1, tiled=True),
        lax.all_to_all(
            row_dots.reshape(local_experts, group_count, CAP),
            "expert",
            split_axis=1,
            concat_axis=1,
            tiled=True,
        ),
    )
    choice_grad = (
        ret_grad.reshape(slot_total, channels)[destination]
        .astype(jnp.float32)
        .reshape(tokens, TOP, channels)
    )
    norm_grad = jnp.sum(choice_grad, axis=1)
    inner_mean = jnp.mean(norm_grad * norm_float, axis=-1, keepdims=True)
    residual_grad = (
        cot_rows.astype(jnp.float32) + (norm_grad - norm_float * inner_mean) / rms_value
    ).astype(jnp.bfloat16)
    choice_dots = ret_dots.reshape(slot_total)[destination].astype(jnp.float32).reshape(tokens, TOP)
    gate_drive = keep_float * choice_dots
    gate_mix = jnp.sum(gates_top * gate_drive, axis=-1, keepdims=True)
    gate_part = gates_top * (gate_drive - gate_mix)
    logit_gate = jnp.sum(jnp.where(one_hot, gate_part[:, :, None], 0.0), axis=1)
    expert_share = jnp.sum(jnp.where(one_hot, keep_float[:, :, None], 0.0), axis=(0, 1)) / (
        TOP * tokens
    )
    logit_max = jnp.max(router_logits, axis=-1, keepdims=True)
    logit_exp = jnp.exp(router_logits - logit_max)
    router_probs = logit_exp / jnp.sum(logit_exp, axis=-1, keepdims=True)
    share_mean = jnp.sum(router_probs * expert_share[None, :], axis=-1, keepdims=True)
    balance = EXPERTS * router_probs * (expert_share[None, :] - share_mean)
    logit_grad = (logit_gate + balance).reshape(1, win_side, map_width, EXPERTS)
    grad_map = residual_grad.reshape(win_side, map_width, channels)
    next_grad = from_behind(grad_map[:half_win], "space", -1)
    grad_shifted = jnp.concatenate([grad_map[half_win:], next_grad], axis=0)
    last_flags = jnp.reshape(space_index == space_count - 1, (1,))
    frame_grads = window_grads(qkv_shifted[:, None], grad_shifted[None], last_flags, HEADS)[:, 0]
    prev_rows = from_behind(frame_grads[:, half_win:], "space", 1)
    attn_grad = jnp.concatenate([prev_rows, frame_grads[:, :half_win]], axis=1)
    return (attn_grad[:, None], grad_map[None], up_total, down_total, logit_grad)


META = 8
PAD = 16
GELU_C = math.sqrt(2.0 / math.pi)
GELU_A = 0.044715


def iota(shape, dim):
    return lax.broadcasted_iota(jnp.int32, shape, dim)


def dot(a, b, ca, cb):
    return lax.dot_general(a, b, (((ca,), (cb,)), ((), ())), preferred_element_type=jnp.float32)


def to_lanes(column):
    n = column.shape[0]
    return jnp.sum(jnp.where(iota((n, n), 0) == iota((n, n), 1), column, 0.0), axis=0, keepdims=True)


def to_rows(row):
    n = row.shape[1]
    return jnp.sum(jnp.where(iota((n, n), 0) == iota((n, n), 1), row, 0.0), axis=1, keepdims=True)


def stack_rows(rows):
    out = jnp.zeros((META, rows[0].shape[1]), jnp.float32)
    sub = iota(out.shape, 0)
    for k, row in enumerate(rows):
        out = jnp.where(sub == k, row, out)
    return out


def split_hi_lo(x):
    hi = x.astype(jnp.bfloat16).astype(jnp.float32)
    return hi, x - hi


def routing(logits, ids):
    cols = iota(logits.shape, 1).astype(jnp.float32)
    hot = [cols == ids[k] for k in range(TOP)]
    z = [jnp.sum(jnp.where(h, logits, 0.0), axis=-1, keepdims=True) for h in hot]
    top = jnp.maximum(z[0], z[1])
    ex = [jnp.exp(v - top) for v in z]
    total = ex[0] + ex[1]
    return hot, [v / total for v in ex]


def flatten(ref, rows_ref, first=0, count=None):
    side = ref.shape[1]
    for i in range(count or ref.shape[0]):
        rows_ref[i * side : (i + 1) * side, :] = ref[first + i].astype(jnp.float32)


def column(ref, k):
    rows, _, side = ref.shape
    line = iota((rows * side, rows), 0)
    spread = jnp.where(line // side == iota((rows * side, rows), 1), 1.0, 0.0).astype(jnp.bfloat16)
    wide = dot(spread, ref[:, k, :].astype(jnp.float32).astype(jnp.bfloat16), 1, 0)
    own = iota(wide.shape, 0) % side == iota(wide.shape, 1)
    return jnp.sum(jnp.where(own, wide, 0.0), axis=1, keepdims=True)


def halve_kernel(x_ref, up_ref, low_ref, rows_ref):
    side = x_ref.shape[1] // 2
    for n in range(x_ref.shape[0]):
        for at, out in ((0, up_ref), (side, low_ref)):
            flatten(x_ref.at[n], rows_ref, at, side)
            out[n] = rows_ref[...].astype(jnp.bfloat16)


def prep_kernel(res_ref, log_ref, ids_ref, keep_ref, cot_ref, out_ref, flat_ref, cols_ref, rows_ref):
    tokens, channels = rows_ref.shape
    flatten(cot_ref, rows_ref)
    out_ref[1, :tokens, :] = rows_ref[...].astype(jnp.bfloat16)
    flatten(res_ref, rows_ref)
    res = rows_ref[...]
    flat_ref[...] = res.astype(jnp.bfloat16)
    rms = jnp.sqrt(jnp.mean(res * res, axis=-1, keepdims=True) + NORM_EPS)
    out_ref[0, :tokens, :] = (res / rms).astype(jnp.bfloat16)
    cols = [column(ref, k) for ref in (ids_ref, keep_ref) for k in range(TOP)]
    lane = iota(cols_ref.shape, 1)
    table = jnp.zeros(cols_ref.shape, jnp.float32)
    for n, c in enumerate(cols):
        table = jnp.where(lane == n, c, table)
    cols_ref[...] = table
    ids, keep = cols[:TOP], cols[TOP:]
    hot, gates = routing(log_ref[...], ids)
    both = jnp.where(hot[0] | hot[1], 1.0, 0.0).astype(jnp.bfloat16)
    earlier = jnp.where(iota((tokens, tokens), 1) < iota((tokens, tokens), 0), 1.0, 0.0)
    count = dot(earlier.astype(jnp.bfloat16), both, 1, 0)
    where, weight = [], []
    for k in range(TOP):
        slot = jnp.sum(jnp.where(hot[k], count, 0.0), axis=-1, keepdims=True)
        where += [ids[k], slot]
        weight += split_hi_lo(gates[k] * keep[k])
    for side, cols in ((0, where), (1, weight)):
        out_ref[side, tokens:, :] = jnp.zeros((META, channels), jnp.bfloat16)
        rows = stack_rows([to_lanes(c) for c in cols])
        out_ref[side, tokens:, :tokens] = rows.astype(jnp.bfloat16)


def ffn_kernel(table, tokens, base_ref, *refs):
    used = 1 + max(max(t[0], t[2]) for t in table)
    tok_refs = refs[:used]
    up_ref, down_ref = refs[used : used + 2]
    mine_ref, part_ref, x_ref, pg_ref, ag_ref = refs[used + 2 : used + 7]
    xs, gs, ds, rs = refs[used + 7 :]
    rows = xs.shape[1]
    channels = up_ref.shape[1]
    half = channels // 2
    step = pl.program_id(0)
    strips = [(tok_refs[a], i, tok_refs[b], j, who, to) for a, i, b, j, who, to in table]

    def choices(ref, n_at):
        meta = ref[n_at, tokens:, :].astype(jnp.float32)[:, :tokens]
        base = base_ref[0].astype(jnp.float32)
        line = iota((rows, tokens), 0).astype(jnp.float32)
        return [
            line == (meta[2 * k : 2 * k + 1] - base) * PAD + meta[2 * k + 1 : 2 * k + 2]
            for k in range(TOP)
        ]

    @pl.when(step == 0)
    def _():
        for i, (ref, n_at, cref, c_at, _, _) in enumerate(strips):
            picks = choices(ref, n_at)
            pick = jnp.where(picks[0] | picks[1], 1.0, 0.0).astype(jnp.bfloat16)
            gate = cref[c_at, tokens:, :].astype(jnp.float32)[:, :tokens]
            xs[i, :, :channels] = dot(pick, ref[n_at, :tokens, :], 1, 0).astype(jnp.bfloat16)
            xs[i, :, channels:] = dot(pick, cref[c_at, :tokens, :], 1, 0).astype(jnp.bfloat16)
            weight = sum(
                jnp.where(picks[k], gate[2 * k : 2 * k + 1] + gate[2 * k + 1 : 2 * k + 2], 0.0)
                for k in range(TOP)
            )
            gs[i] = jnp.sum(weight, axis=1, keepdims=True)

    count = len(strips) * PAD
    batch = x_ref.shape[0]
    for b in range(batch):
        e = step * batch + b
        at = pl.ds(pl.multiple_of(e * PAD, PAD), PAD)
        x = xs[:, at, :].reshape(count, 2 * channels)
        g = gs[:, at, :].reshape(count, 1)
        x_ref[b] = x
        pre = dot(x[:, :channels], up_ref[b], 1, 0)
        drive = dot(x[:, channels:], down_ref[b], 1, 0)
        sq = pre * pre
        t = jnp.tanh(pre * (GELU_C + (GELU_C * GELU_A) * sq))
        low = 0.5 + 0.5 * t
        act = pre * low
        slope = low + act * (1.0 - t) * (GELU_C + (3.0 * GELU_C * GELU_A) * sq)
        dots = jnp.sum(act.astype(jnp.bfloat16).astype(jnp.float32) * drive, axis=1, keepdims=True)
        ds[:, at, :] = dots.reshape(len(strips), PAD, 1)
        ag_ref[b] = (g * act).astype(jnp.bfloat16)
        pg = (g * drive * slope).astype(jnp.bfloat16)
        pg_ref[b] = pg
        back = dot(pg, up_ref[b], 1, 1).astype(jnp.bfloat16)
        rs[:, at, :] = back.reshape(len(strips), PAD, channels)

    @pl.when(step == pl.num_programs(0) - 1)
    def _():
        for i, (ref, n_at, _, _, who, to) in enumerate(strips):
            picks = choices(ref, n_at)
            pick = jnp.where(picks[0] | picks[1], 1.0, 0.0).astype(jnp.bfloat16)
            grad = dot(pick, rs[i], 0, 0).astype(jnp.bfloat16)
            d = [jnp.sum(jnp.where(p, ds[i], 0.0), axis=0, keepdims=True) for p in picks]
            d = [split_hi_lo(v) for v in d]
            out = mine_ref if who == 0 else part_ref
            for h in range(2):
                out[h, to, :tokens, :] = grad[:, h * half : (h + 1) * half]
                out[h, to, tokens:, :] = jnp.zeros((META, half), jnp.bfloat16)
            rows_d = stack_rows([d[0][0], d[1][0], d[0][1], d[1][1]])
            out[0, to, tokens:, :tokens] = rows_d.astype(jnp.bfloat16)


def run_ffn(base, toks, table, up, down, tokens):
    experts, channels, hidden = up.shape
    strips = len(table)
    count = strips * PAD
    half = channels // 2
    whole = lambda shape: pl.BlockSpec(
        shape, lambda j: (0,) * len(shape), pipeline_mode=pl.Buffered(1)
    )
    each = lambda shape: pl.BlockSpec((FFN_BATCH,) + shape, lambda j: (j,) + (0,) * len(shape))
    out_t = (2, strips // 2, tokens + META, half)
    bf = jnp.bfloat16
    return pl.pallas_call(
        functools.partial(ffn_kernel, table, tokens),
        grid=(experts // FFN_BATCH,),
        out_shape=[
            jax.ShapeDtypeStruct(out_t, bf),
            jax.ShapeDtypeStruct(out_t, bf),
            jax.ShapeDtypeStruct((experts, count, 2 * channels), bf),
            jax.ShapeDtypeStruct((experts, count, hidden), bf),
            jax.ShapeDtypeStruct((experts, count, hidden), bf),
        ],
        in_specs=[pl.BlockSpec(memory_space=pltpu.SMEM)]
        + [pl.BlockSpec(memory_space=pltpu.VMEM)] * len(toks)
        + [each((channels, hidden))] * 2,
        out_specs=[
            whole(out_t),
            whole(out_t),
            each((count, 2 * channels)),
            each((count, hidden)),
            each((count, hidden)),
        ],
        scratch_shapes=[
            pltpu.VMEM((strips, experts * PAD, 2 * channels), bf),
            pltpu.VMEM((strips, experts * PAD, 1), jnp.float32),
            pltpu.VMEM((strips, experts * PAD, 1), jnp.float32),
            pltpu.VMEM((strips, experts * PAD, channels), bf),
        ],
        compiler_params=pltpu.CompilerParams(dimension_semantics=("arbitrary",), vmem_limit_bytes=40 << 20),
        cost_estimate=pl.CostEstimate(
            flops=12 * experts * count * channels * hidden,
            bytes_accessed=8 * up.size + count * 4096 * experts,
            transcendentals=0,
        ),
        name="ffn",
    )(base, *map(near, toks), up, down)


def wgrad_kernel(n, keep, *refs):
    refs = refs[keep:]
    xs, pgs, ags = refs[:n], refs[n : 2 * n], refs[2 * n : 3 * n]
    up_ref, down_ref = refs[3 * n :]
    channels = up_ref.shape[1]
    x = jnp.concatenate([a[0] for a in xs], axis=0)
    up_ref[0] = dot(x[:, :channels], jnp.concatenate([a[0] for a in pgs], axis=0), 0, 0)
    down_ref[0] = dot(x[:, channels:], jnp.concatenate([a[0] for a in ags], axis=0), 0, 0)


def run_wgrad(xs, pgs, ags, first, last, before=()):
    experts, _, two = xs[0].shape
    hidden = pgs[0].shape[2]
    each = lambda shape: pl.BlockSpec((1,) + shape[1:], lambda j: (j + first, 0, 0))
    out = (experts, two // 2, hidden)
    ops = list(xs) + list(pgs) + list(ags)
    rows = sum(x.shape[1] for x in xs)
    return pl.pallas_call(
        functools.partial(wgrad_kernel, len(xs), len(before)),
        grid=(last - first,),
        out_shape=[jax.ShapeDtypeStruct(out, jnp.float32)] * 2,
        in_specs=[pl.BlockSpec(memory_space=pl.ANY)] * len(before) + [each(a.shape) for a in ops],
        out_specs=[each(out)] * 2,
        input_output_aliases={i: i for i in range(len(before))},
        compiler_params=pltpu.CompilerParams(dimension_semantics=("arbitrary",)),
        cost_estimate=pl.CostEstimate(
            flops=2 * (last - first) * rows * two * hidden,
            bytes_accessed=(last - first) * (sum(a.size * 2 for a in ops) // experts + 4 * two * hidden),
            transcendentals=0,
        ),
        name="wgrad",
    )(*before, *ops)


def add_blocks(a, b, tokens):
    s = a.astype(jnp.float32) + b.astype(jnp.float32)
    return s[:tokens].astype(jnp.bfloat16), meta_sum(s[tokens:]).astype(jnp.bfloat16)


def meta_sum(s):
    total = s + pltpu.roll(s, META - TOP, 0)
    hi, lo = split_hi_lo(total)
    sub = iota(s.shape, 0)
    return jnp.where(sub < TOP, hi, jnp.where(sub < 2 * TOP, pltpu.roll(lo, TOP, 0), 0.0))


def put(ref, at, a, b, tokens):
    body, meta = add_blocks(a, b, tokens)
    ref[at, :tokens, :] = body
    ref[at, tokens:, :] = meta


def core_sum_kernel(chunks, tokens, mine_ref, got_ref, k1_ref, s1_ref, k2_ref, s2_ref):
    for c in range(chunks):
        for y in range(2):
            for x in range(2):
                i = c * 4 + y * 2 + x
                put((k1_ref, s1_ref)[x], c * 2 + y, mine_ref[0, i], got_ref[0, i], tokens)
                put((k2_ref, s2_ref)[y], c * 2 + x, mine_ref[1, i], got_ref[1, i], tokens)


def pair_sum_kernel(chunks, tokens, a1, b1, a2, b2, k1_ref, s1_ref, k2_ref, s2_ref):
    for c in range(chunks):
        for u in range(2):
            i = c * 2 + u
            put((k1_ref, s1_ref)[u], c, a1[i], b1[i], tokens)
            put((k2_ref, s2_ref)[u], c, a2[i], b2[i], tokens)


def last_sum_kernel(tokens, a1, b1, a2, b2, *outs):
    for c, ref in enumerate(outs):
        put(ref, 0, a1[c], b1[c], tokens)
        put(ref, 1, a2[c], b2[c], tokens)


def near(a):
    return pltpu.with_memory_space_constraint(a, pltpu.VMEM)


def vmem_call(kernel, outs, *ops, scratch=(), far=0):
    full = pl.BlockSpec(memory_space=pltpu.VMEM)
    size = sum(a.size * a.dtype.itemsize for a in list(ops) + list(outs))
    return pl.pallas_call(
        kernel,
        out_shape=outs,
        in_specs=[full] * len(ops),
        out_specs=[full] * len(outs),
        scratch_shapes=list(scratch),
        compiler_params=pltpu.CompilerParams(vmem_limit_bytes=16 << 20),
        cost_estimate=pl.CostEstimate(flops=size, bytes_accessed=size, transcendentals=0),
    )(*[near(a) if i >= far else a for i, a in enumerate(ops)])


def final_kernel(n, res_ref, blk_ref, log_ref, cols_ref, *refs):
    parts = refs[:n]
    up_ref, low_ref, map_ref, log_out, rows_ref = refs[n:]
    tokens, _ = res_ref.shape
    res = res_ref[...].astype(jnp.float32)
    rms = jnp.sqrt(jnp.mean(res * res, axis=-1, keepdims=True) + NORM_EPS)
    nf = res / rms
    halves = [sum(p[h].astype(jnp.float32) for p in parts) for h in range(2)]
    grad = jnp.concatenate([h[:tokens] for h in halves], axis=1)
    inner = jnp.mean(grad * nf, axis=-1, keepdims=True)
    cot = blk_ref[1, :tokens, :].astype(jnp.float32)
    out = cot + (grad - nf * inner) / rms
    mid = tokens // 2
    up_ref[...] = out[:mid].astype(jnp.bfloat16)
    low_ref[...] = out[mid:].astype(jnp.bfloat16)
    rows_ref[...] = out
    side = map_ref.shape[1]
    for i in range(map_ref.shape[0]):
        map_ref[i] = rows_ref[i * side : (i + 1) * side, :].astype(jnp.bfloat16)
    meta = halves[0][tokens:]
    total = (meta + pltpu.roll(meta, META - TOP, 0))[:, :tokens]
    logits = log_ref[...]
    experts = logits.shape[1]
    cols = [cols_ref[:, k : k + 1] for k in range(2 * TOP)]
    keeps = cols[TOP:]
    hot, gates = routing(logits, cols[:TOP])
    dots = [to_rows(total[k : k + 1]).astype(jnp.bfloat16).astype(jnp.float32) for k in range(TOP)]
    drive = [keeps[k] * dots[k] for k in range(TOP)]
    mix = gates[0] * drive[0] + gates[1] * drive[1]
    part = sum(jnp.where(hot[k], gates[k] * (drive[k] - mix), 0.0) for k in range(TOP))
    share = sum(
        jnp.sum(jnp.where(hot[k], keeps[k], 0.0), axis=0, keepdims=True) for k in range(TOP)
    ) / (TOP * tokens)
    top = jnp.max(logits, axis=-1, keepdims=True)
    ex = jnp.exp(logits - top)
    probs = ex / jnp.sum(ex, axis=-1, keepdims=True)
    mean = jnp.sum(probs * share, axis=-1, keepdims=True)
    log_out[...] = part + experts * probs * (share - mean)


def attn_kernel(heads, side, at_ref, up, low, after, before, gu, gl, gafter, gbefore, out_ref):
    mid, width = gu.shape
    area = 2 * mid
    dim = width // heads
    inv = dim**-0.5
    first = pl.program_id(0) == 0
    wide = lambda r: r.astype(jnp.float32)
    window = lambda l, a, b, u: jnp.concatenate(
        [jnp.where(first, wide(l), wide(b)), jnp.where(first, wide(a), wide(u))], axis=0
    ).astype(jnp.bfloat16)
    q, k, v = [window(low[n], after[n], before[n], up[n]) for n in range(3)]
    g = window(gl[...], gafter[...], gbefore[...], gu[...])
    lane = iota((area, width), 1) // dim
    masks = [jnp.where(lane == h, 1.0, 0.0) for h in range(heads)]
    spread = lambda a: jnp.concatenate([a * m.astype(jnp.bfloat16) for m in masks], axis=0)
    qs, gsp = spread(q), spread(g)
    last = jnp.where(first, at_ref[0], at_ref[1]).astype(jnp.float32)

    def label(at):
        at = at % area
        col = jnp.where(at % side >= side // 2, 1.0, 0.0)
        return col + jnp.where(at >= mid, 2.0 * last, 0.0)

    away = label(iota((area, 1), 0)) != label(iota((1, heads * area), 1))
    scores = dot(k, qs, 1, 1) * inv + jnp.where(away, SCORE_MASK, 0.0)
    ex = jnp.exp(scores - jnp.max(scores, axis=0, keepdims=True))
    probs = ex * (1.0 / jnp.sum(ex, axis=0, keepdims=True))
    weights = probs.astype(jnp.bfloat16)
    pgrad = dot(v, gsp, 1, 1)
    delta = jnp.sum(weights.astype(jnp.float32) * pgrad, axis=0, keepdims=True)
    sgrad = (probs * (pgrad - delta)).astype(jnp.bfloat16)
    dk = dot(sgrad, qs, 1, 0) * inv
    dv = dot(weights, gsp, 1, 0)
    broad = dot(sgrad, k, 0, 0)
    dq = sum(broad[h * area : (h + 1) * area] * masks[h] for h in range(heads)) * inv
    for n, a in enumerate((dq, dk, dv)):
        own = jnp.where(first, a[:mid], a[mid:])
        for i in range(mid // side):
            out_ref[n, i] = own[i * side : (i + 1) * side].astype(jnp.bfloat16)


def run_attention(at, halves, grads, side, groups):
    _, mid, channels = halves[0].shape
    width = channels // groups
    heads = HEADS // groups
    rows = mid // side
    return pl.pallas_call(
        functools.partial(attn_kernel, heads, side),
        grid=(2, groups),
        out_shape=jax.ShapeDtypeStruct((3, 2 * rows, side, channels), jnp.bfloat16),
        in_specs=[pl.BlockSpec(memory_space=pltpu.SMEM)]
        + [pl.BlockSpec((3, mid, width), lambda w, g: (0, 0, g))] * 4
        + [pl.BlockSpec((mid, width), lambda w, g: (0, g))] * 4,
        out_specs=pl.BlockSpec((3, rows, side, width), lambda w, g: (0, 1 - w, 0, g)),
        compiler_params=pltpu.CompilerParams(dimension_semantics=("arbitrary", "arbitrary")),
        cost_estimate=pl.CostEstimate(
            flops=40 * mid * mid * channels * heads, bytes_accessed=64 * mid * channels, transcendentals=0
        ),
        name="attn",
    )(at, *halves, *grads)


def per_device_tokens(
    attn_inputs, residual, logits, expert_ids, keep_mask, cotangent, up_weight, down_weight
):
    n_exp, n_space = lax.axis_size("expert"), lax.axis_size("space")
    local = up_weight.shape[0]
    win_side, map_width, channels = residual.shape[1:]
    tokens = win_side * map_width
    mid = tokens // 2
    deep = n_space // 2

    def send(block, dz=0, dx=0, dy=0, dc=0):
        pairs = []
        for e in range(n_exp):
            for s in range(n_space):
                y, c, z, x = e // 2, e % 2, s // 2, s % 2
                to_e = (y + dy) % (n_exp // 2) * 2 + (c + dc) % 2
                to_s = (z + dz) % deep * 2 + (x + dx) % 2
                pairs.append((e * n_space + s, to_e * n_space + to_s))
        return lax.ppermute(block, ("expert", "space"), pairs)

    def neighbour(block, distance):
        return from_behind(block, "space", distance)

    bf = jnp.bfloat16
    deal = jax.ShapeDtypeStruct
    rows = tokens + META
    half = channels // 2
    third = deal((3, mid, channels), bf)
    q_up, q_low = vmem_call(
        halve_kernel, [third, third], attn_inputs[:, 0],
        scratch=[pltpu.VMEM((mid, channels), jnp.float32)], far=1,
    )
    q_after = neighbour(q_up, -1)
    q_before = neighbour(q_low, 1)
    log = logits[0].reshape(tokens, EXPERTS)
    turned = lambda a: a[0].transpose(0, 2, 1)
    flat_rows = pltpu.VMEM((tokens, channels), jnp.float32)
    block, flat, cols = vmem_call(
        prep_kernel,
        [deal((2, rows, channels), bf), deal((tokens, channels), bf), deal((tokens, META), jnp.float32)],
        residual[0], log, turned(expert_ids), turned(keep_mask), cotangent[0],
        scratch=[flat_rows], far=5,
    )

    base = jnp.reshape(lax.axis_index("expert") * local, (1,)).astype(jnp.int32)
    moved = [block] + [send(block, dz=d) for d in range(1, deep)]
    xs, pgs, ags, parts = [], [], [], []
    for group in (range(deep - 1), range(deep - 1, deep)):
        toks, table = [], []
        for c, d in enumerate(group):
            own = moved[d]
            x = send(own, dx=1)
            y = send(own, dy=1)
            if d == deep - 1:
                diag = [send(x[:1], dy=1), send(y[1:], dx=1)]
            else:
                diag = [send(x, dy=1) if d % 2 == 0 else send(y, dx=1)]
            for who in range(2):
                got = [own, x, y] + diag
                if who:
                    got = [send(a, dc=1) for a in got]
                at, to = len(toks), 4 * c
                toks += got
                table += [(at + i, 0, at + i, 1, who, to + i) for i in range(3)]
                table.append((at + 3, 0, at + 2 + len(diag), 1 if len(diag) == 1 else 0, who, to + 3))
        t_mine, t_part, xd, pg, ag = run_ffn(base, toks, table, up_weight, down_weight, tokens)
        xs.append(xd)
        pgs.append(pg)
        ags.append(ag)
        got = send(t_part, dc=1)
        n = len(group)
        two = deal((2 * n, rows, half), bf)
        k1, s1, k2, s2 = vmem_call(
            functools.partial(core_sum_kernel, n, tokens),
            [two] * 4,
            t_mine, got,
        )
        r1, r2 = send(s1, dx=1), send(s2, dy=1)
        one = deal((n, rows, half), bf)
        k1, s1, k2, s2 = vmem_call(
            functools.partial(pair_sum_kernel, n, tokens), [one] * 4, k1, r1, k2, r2
        )
        r1, r2 = send(s1, dy=1), send(s2, dx=1)
        done = vmem_call(
            functools.partial(last_sum_kernel, tokens),
            [deal((2, rows, half), bf)] * n,
            k1, r1, k2, r2,
        )
        for d, w in zip(group, done):
            parts.append(w if d == 0 else send(w, dz=-d))
    cuts = [local * i // WGRAD_PIECES for i in range(WGRAD_PIECES + 1)]
    totals = ()
    for i in range(WGRAD_PIECES):
        totals = run_wgrad(xs, pgs, ags, cuts[i], cuts[i + 1], totals)

    g_up, g_low, g_map, logit_grad = vmem_call(
        functools.partial(final_kernel, deep),
        [deal((mid, channels), bf)] * 2
        + [deal((win_side, map_width, channels), bf), deal((tokens, EXPERTS), jnp.float32)],
        flat, block, log, cols, *parts,
        scratch=[flat_rows], far=4,
    )
    g_after = neighbour(g_up, -1)
    g_before = neighbour(g_low, 1)
    space = lax.axis_index("space")
    last = jnp.stack([space == n_space - 1, space == 0]).astype(jnp.int32)
    grads = run_attention(
        last, (q_up, q_low, q_after, q_before), (g_up, g_low, g_after, g_before), map_width, 2
    )
    return (
        grads[:, None],
        g_map[None],
        *totals,
        logit_grad.reshape(1, win_side, map_width, EXPERTS),
    )


WGRAD_PIECES = 3
FFN_BATCH = 4


def solution(mesh):
    n_exp, n_space = mesh.shape["expert"], mesh.shape["space"]
    local = EXPERTS // n_exp
    gather_tokens = n_exp // 2 == 2 and n_space % 2 == 0 and n_space // 2 == 4 and 2 * local * CAP >= TOKENS

    def per_device(*args):
        return per_device_tokens(*args)

    in_specs = (
        P(None, "expert", "space", None, None),
        P("expert", "space", None, None),
        P("expert", "space", None, None),
        P("expert", "space", None, None),
        P("expert", "space", None, None),
        P("expert", "space", None, None),
        P("expert", None, "space"),
        P("expert", None, "space"),
    )
    out_specs = (
        P(None, "expert", "space", None, None),
        P("expert", "space", None, None),
        P("expert", None, "space"),
        P("expert", None, "space"),
        P("expert", "space", None, None),
    )
    return jax.shard_map(
        per_device if gather_tokens else per_device_slots,
        mesh=mesh, in_specs=in_specs, out_specs=out_specs, check_vma=False,
    )
```
